512 devices in a mesh: node: 64 (over y_lo, z, core), win: 8 (over y_hi, x).
Axes of the slice: x: 4, y: 8 (y_hi: 2, y_lo: 4; y = y_hi * 4 + y_lo), z: 8, core: 2. Of those that a mesh axis runs over, the one named last changes fastest.
Arguments:
- features: bfloat16 [32768, 8, 2, 128], P('node', 'win'), may hold values from -6 to 6
- node_vectors: float32 [32768, 128], P('node'), may hold values from -0.3 to 0.3
- projections: float32 [2, 64, 64], replicated, may hold values from -0.75 to 0.75
- mix_weight: bfloat16 [3, 128, 128], replicated, may hold values from -0.3125 to 0.3125
- region_sizes: int32 [128], replicated, may hold values from 1 to 4, 256 in all
- cotangent: bfloat16 [32768, 8, 2, 128], P('node', 'win'), may hold values from -6 to 6
Outputs:
- layer_output: bfloat16 [32768, 8, 2, 128], P('node', 'win')
- vector_grad: float32 [32768, 128], P('node')
- weight_grad: float32 [3, 128, 128], replicated
The draws below stay inside these ranges and needn't reach their ends.
Inputs may be any that keep to these rules, and one draw needn't show every extreme that they name: `region_sizes`: each entry is a region size in units of 128 nodes; the entries sum to 256, and the largest region has 512 nodes.
All inputs are finite; a program needn't handle non-finite values.
Results may differ from the reference program's by a relative error of at most 0.015.
Values may be sent and summed in bfloat16 or wider, within the bound.
No kernel may reach another device: no remote copies, remote signals or barrier semaphores. Data moves between devices by JAX's collectives and lax.ppermute only.
A program may use at most 64 MiB of HBM per device.

```python
import math
import jax
import jax.numpy as jnp
import numpy as np
from jax import lax

C = 128
EMB = 64
STEPS = 2
HOPS = 2
BLOCK = 128
NODE_DEV = 512
NODES = 32768
WINDOWS = 8
REGIONS = 128


def block_scale(stream_key, dims, cuts, low, high):
    loudness, own = 1.0, jax.random.fold_in(stream_key, 6)
    for position, shards_of in cuts:
        steps = jnp.exp(jax.random.uniform(jax.random.fold_in(own, position), (shards_of,), jnp.float32, low / len(cuts), high / len(cuts)))
        loudness = loudness * jnp.repeat(steps, dims[position] // shards_of).reshape([-1 if axis == position else 1 for axis in range(len(dims))])
    return loudness


def split_up(number_of, total, limit, lean):
    portions = [(1 << 20) // math.isqrt(rank ** lean) + 1 for rank in range(2, number_of + 1)]
    spare, counts = total - limit - (number_of - 1), [1] * (number_of - 1)
    while spare > 0:
        movable = [i for i in range(number_of - 1) if counts[i] < limit]
        whole, remaining = sum([portions[i] for i in movable]), spare
        for i in movable:
            extra = min(limit - counts[i], max(1, remaining * portions[i] // whole), spare)
            counts[i] = counts[i] + extra
            spare = spare - extra
    return np.array([limit] + counts)


def ragged(rng, number_of, total, reach, skew):
    if number_of == 2:
        one = jax.random.randint(rng, (), max(1, total - reach), min(reach, total - 1) + 1)
        return jnp.stack([one, total - one])
    tallies = jnp.asarray(split_up(number_of, total, reach, skew), jnp.int32)
    couples = (number_of - 1) // 2
    source_of, receiver = tallies[1:1 + 2 * couples:2], tallies[2:2 + 2 * couples:2]
    margin = jnp.minimum(source_of - 1, reach - receiver)
    passed = jax.random.randint(jax.random.fold_in(rng, 1), (couples,), 0, 1 << 20) % (margin + 1)
    tallies = tallies.at[1:1 + 2 * couples:2].set(source_of - passed).at[2:2 + 2 * couples:2].set(receiver + passed)
    return tallies[jax.random.permutation(jax.random.fold_in(rng, 2), number_of)]


def normal_values(rng, shape, deviation, bound, split=(), held_as=jnp.bfloat16):
    result = jax.random.normal(rng, shape, jnp.float32) * deviation
    if len(split) > 0:
        result = block_scale(rng, shape, split, -0.22, 0.18) * result
    return jnp.clip(result, min=-bound, max=bound).astype(held_as)


def setup_inputs(seed: int = 0) -> dict:
    key_of = jax.random.split(jax.random.key(seed), 7)
    features = normal_values(key_of[0], (NODES, WINDOWS, STEPS, C), 1.0, 6.0, ((0, 64), (1, 8)))
    node_vectors = normal_values(key_of[1], (NODES, 2 * EMB), 0.05, 0.3, ((0, 64),), jnp.float32)
    projections = normal_values(key_of[2], (2, EMB, EMB), EMB ** -0.5, 0.75, (), jnp.float32)
    mix_weight = normal_values(key_of[3], (HOPS + 1, C, C), (C * (HOPS + 1)) ** -0.5, 0.3125)
    region_sizes = ragged(key_of[4], REGIONS, NODES // BLOCK, NODE_DEV // BLOCK, 2).astype(jnp.int32)
    cotangent = normal_values(key_of[5], (NODES, WINDOWS, STEPS, C), 1.0, 6.0, ((0, 64), (1, 8)))
    return dict(features=features, node_vectors=node_vectors, projections=projections, mix_weight=mix_weight, region_sizes=region_sizes, cotangent=cotangent)


KEEP_INPUT = 0.05
ROWS_DIMS = (((1,), (1,)), ((), ()))
COLS_DIMS = (((0,), (0,)), ((), ()))

def swapped(vectors):
    emb_half = vectors.shape[1] // 2
    return jnp.concatenate([vectors[:, emb_half:], -vectors[:, :emb_half]], axis=1)

def node_regions(region_sizes, node_index):
    region_ends = jnp.cumsum(region_sizes).astype(jnp.int32) * BLOCK
    region_index = lax.optimization_barrier(jnp.sum((region_ends[None, :] <= node_index[:, None]).astype(jnp.int32), axis=1)).astype(jnp.int32)
    in_range = (node_index >= 0) & (node_index < NODES)
    return jnp.where(in_range, region_index, -1).astype(jnp.int32)

def padded(values):
    zero_rows = jnp.zeros((NODE_DEV, values.shape[1]), values.dtype)
    return jnp.concatenate([zero_rows, values, zero_rows], axis=0)

def spread(parts):
    lower = parts[:, :NODE_DEV]
    middle = parts[:, NODE_DEV:2 * NODE_DEV]
    upper = parts[:, 2 * NODE_DEV:]
    zero_block = jnp.zeros_like(lower[:1])
    from_above = jnp.concatenate([lower[1:], zero_block], axis=0)
    from_below = jnp.concatenate([zero_block, upper[:-1]], axis=0)
    return (middle + from_above + from_below).reshape(-1, parts.shape[2])

def reference(features, node_vectors, projections, mix_weight, region_sizes, cotangent):
    row_width = WINDOWS * STEPS * C
    block_count = NODES // NODE_DEV
    block_ids = jnp.arange(block_count, dtype=jnp.int32)
    highest = lax.Precision.HIGHEST
    source_m = jnp.tanh(3.0 * jnp.dot(node_vectors[:, :EMB], projections[0], precision=highest, preferred_element_type=jnp.float32))
    target_m = jnp.tanh(3.0 * jnp.dot(node_vectors[:, EMB:], projections[1], precision=highest, preferred_element_type=jnp.float32))
    learned = jnp.concatenate([source_m, target_m], axis=1).astype(jnp.bfloat16)
    learned_pad = padded(learned)
    region_pad = node_regions(region_sizes, jnp.arange(-NODE_DEV, NODES + NODE_DEV, dtype=jnp.int32))

    def block_graph(block_index):
        first_node = block_index * NODE_DEV
        own_learned = lax.dynamic_slice_in_dim(learned, first_node, NODE_DEV, 0)
        wide_learned = lax.dynamic_slice_in_dim(learned_pad, first_node, 3 * NODE_DEV, 0)
        own_region = lax.dynamic_slice_in_dim(region_pad, first_node + NODE_DEV, NODE_DEV, 0)
        wide_region = lax.dynamic_slice_in_dim(region_pad, first_node, 3 * NODE_DEV, 0)
        scores = lax.dot_general(own_learned, swapped(wide_learned), ROWS_DIMS, preferred_element_type=jnp.float32)
        same_region = (own_region[:, None] == wide_region[None, :]) & (wide_region[None, :] >= 0)
        positive = jnp.maximum(jnp.tanh(3.0 * scores), 0.0)
        adjacency = jnp.where(same_region, positive * positive, 0.0)
        degree = 1.0 + lax.optimization_barrier(jnp.sum(adjacency, axis=1))
        own_index = first_node + jnp.arange(NODE_DEV, dtype=jnp.int32)
        wide_index = first_node - NODE_DEV + jnp.arange(3 * NODE_DEV, dtype=jnp.int32)
        identity = (own_index[:, None] == wide_index[None, :]).astype(jnp.float32)
        adj_rounded = (adjacency + identity).astype(jnp.bfloat16)
        return (scores, same_region, degree, adj_rounded, own_learned, wide_learned)
    degree_all = lax.map(lambda block_index: block_graph(block_index)[2], block_ids).reshape(NODES)

    def propagate(hop_input):
        hop_pad = padded(hop_input)

        def one_block(block_index):
            graph = block_graph(block_index)
            wide_rows = lax.dynamic_slice_in_dim(hop_pad, block_index * NODE_DEV, 3 * NODE_DEV, 0)
            return jnp.dot(graph[3], wide_rows, preferred_element_type=jnp.float32) / graph[2][:, None]
        return lax.map(one_block, block_ids).reshape(NODES, row_width)
    inputs = features.reshape(NODES, row_width)
    inputs_f = inputs.astype(jnp.float32)
    prop_one = propagate(inputs)
    hop_one = (KEEP_INPUT * inputs_f + (1.0 - KEEP_INPUT) * prop_one).astype(jnp.bfloat16)
    prop_two = propagate(hop_one)
    hop_two = (KEEP_INPUT * inputs_f + (1.0 - KEEP_INPUT) * prop_two).astype(jnp.bfloat16)
    row_count = NODES * WINDOWS * STEPS
    hop_list = (inputs, hop_one, hop_two)
    mixed = jnp.zeros((row_count, C), jnp.float32)
    for hop_order in range(3):
        mixed = mixed + jnp.dot(hop_list[hop_order].reshape(row_count, C), mix_weight[hop_order], preferred_element_type=jnp.float32)
    layer_output = mixed.astype(jnp.bfloat16).reshape(features.shape)
    upstream = cotangent.reshape(row_count, C)
    weight_grad = jnp.stack([lax.dot_general(layer_rows.reshape(row_count, C), upstream, COLS_DIMS, preferred_element_type=jnp.float32) for layer_rows in hop_list]) / math.sqrt(row_count)
    back_two = lax.dot_general(upstream, mix_weight[2], ROWS_DIMS, preferred_element_type=jnp.float32).reshape(NODES, row_width)
    grad_two = ((1.0 - KEEP_INPUT) * back_two / degree_all[:, None]).astype(jnp.bfloat16)

    def transposed_block(block_index):
        graph = block_graph(block_index)
        own_grad = lax.dynamic_slice_in_dim(grad_two, block_index * NODE_DEV, NODE_DEV, 0)
        return lax.dot_general(graph[3], own_grad, COLS_DIMS, preferred_element_type=jnp.float32)
    carried = spread(lax.map(transposed_block, block_ids))
    back_one = lax.dot_general(upstream, mix_weight[1], ROWS_DIMS, preferred_element_type=jnp.float32).reshape(NODES, row_width) + carried
    grad_one = ((1.0 - KEEP_INPUT) * back_one / degree_all[:, None]).astype(jnp.bfloat16)
    grad_both = jnp.concatenate([grad_one, grad_two], axis=1)
    hops_pad = padded(jnp.concatenate([inputs, hop_one], axis=1))
    offset = lax.optimization_barrier(jnp.sum(grad_one.astype(jnp.float32) * prop_one, axis=1)) + lax.optimization_barrier(jnp.sum(grad_two.astype(jnp.float32) * prop_two, axis=1))

    def grad_block(block_index):
        scores, same_region, degree, adj_rounded, own_learned, wide_learned = block_graph(block_index)
        own_grad = lax.dynamic_slice_in_dim(grad_both, block_index * NODE_DEV, NODE_DEV, 0)
        wide_hops = lax.dynamic_slice_in_dim(hops_pad, block_index * NODE_DEV, 3 * NODE_DEV, 0)
        pair_inner = lax.dot_general(own_grad, wide_hops, ROWS_DIMS, preferred_element_type=jnp.float32)
        own_offset = lax.dynamic_slice_in_dim(offset, block_index * NODE_DEV, NODE_DEV, 0)
        squashed = jnp.tanh(3.0 * scores)
        positive = jnp.maximum(squashed, 0.0)
        score_grad = jnp.where(same_region, 6.0 * (pair_inner - own_offset[:, None]) * positive * (1.0 - squashed * squashed), 0.0).astype(jnp.bfloat16)
        row_part = jnp.dot(score_grad, swapped(wide_learned), preferred_element_type=jnp.float32)
        column_part = -lax.dot_general(score_grad, swapped(own_learned), COLS_DIMS, preferred_element_type=jnp.float32)
        return (row_part, column_part)
    row_parts, column_parts = lax.map(grad_block, block_ids)
    grad_m = row_parts.reshape(NODES, 2 * EMB) + spread(column_parts)
    source_grad = jnp.dot(3.0 * (1.0 - source_m * source_m) * grad_m[:, :EMB], projections[0].T, precision=highest, preferred_element_type=jnp.float32)
    target_grad = jnp.dot(3.0 * (1.0 - target_m * target_m) * grad_m[:, EMB:], projections[1].T, precision=highest, preferred_element_type=jnp.float32)
    vector_grad = jnp.concatenate([source_grad, target_grad], axis=1)
    return (layer_output, vector_grad, weight_grad)
```

```python
from functools import partial
import math

import jax
import jax.numpy as jnp
from jax import lax
from jax.experimental import pallas as pl
from jax.experimental.pallas import tpu as pltpu
from jax.sharding import PartitionSpec as P

BLOCK = 128
HALO = 3
KEEP_INPUT = 0.05
F32 = jnp.float32
BF16 = jnp.bfloat16
NT = (((1,), (1,)), ((), ()))
TN = (((0,), (0,)), ((), ()))
HIGHEST = lax.Precision.HIGHEST


def block_diagonal(projections):
    zero = jnp.zeros_like(projections[0])
    return jnp.concatenate(
        [
            jnp.concatenate([projections[0], zero], axis=1),
            jnp.concatenate([zero, projections[1]], axis=1),
        ],
        axis=0,
    )


def pack_kernel(x_ref, g_ref, nv_ref, proj_ref, head_ref, tail_ref, m_ref, flat_ref):
    nodes, width = nv_ref.shape
    rim = head_ref.shape[0]
    learned = jnp.tanh(
        3.0
        * jnp.dot(
            nv_ref[...],
            block_diagonal(proj_ref[...]),
            precision=HIGHEST,
            preferred_element_type=F32,
        )
    )
    m_ref[...] = learned
    rounded = learned.astype(BF16)
    head_ref[:, 4 * width :] = rounded[:rim]
    tail_ref[:, 4 * width :] = rounded[nodes - rim :]
    for part, source in enumerate((x_ref, g_ref)):
        flat_ref[...] = source[...].astype(F32)
        for step in range(2):
            rows = flat_ref[pl.ds(step, nodes, stride=2), :].astype(BF16)
            columns = pl.ds((2 * part + step) * width, width)
            head_ref[:, columns] = rows[:rim]
            tail_ref[:, columns] = rows[nodes - rim :]


def layer_kernel(
    norm_scale,
    region_ref,
    low_ref,
    high_ref,
    head_ref,
    tail_ref,
    m_ref,
    proj_ref,
    mix_ref,
    out_ref,
    sums_ref,
    x_ref,
    g_ref,
    learned_ref,
    swapped_ref,
    adj_ref,
    adjt_ref,
    score_ref,
    rdeg_ref,
    one_ref,
    q_one_ref,
    q_two_ref,
    off_ref,
    offrow_ref,
    flat_ref,
):
    b = BLOCK
    nodes, width = m_ref.shape
    rim = head_ref.shape[0]
    own_units = nodes // b
    units = own_units + 2 * HALO
    row = 2 * width
    pieces = (
        (0, low_ref, 0, rim),
        (rim, head_ref, 0, rim),
        (2 * rim, tail_ref, 2 * rim - nodes, nodes - rim),
        (rim + nodes, high_ref, 0, rim),
    )
    for start, source, first, count in pieces:
        x_ref[start : start + count, :] = source[first : first + count, :row]
        g_ref[start : start + count, :] = source[first : first + count, row : 2 * row]
        learned_ref[start : start + count, :] = source[first : first + count, 2 * row :]
    learned = learned_ref[...]
    half = width // 2
    swapped_ref[...] = jnp.concatenate([learned[:, half:], -learned[:, :half]], axis=1)

    chunks = []
    for k in range(units // 2):
        first = max(0, 2 * k - HALO)
        last = min(units - 1, 2 * k + 1 + HALO)
        chunks.append((2 * k, first, last - first + 1))

    def lanes(unit_first, unit_count):
        return slice(unit_first * b, (unit_first + unit_count) * b)

    regions = [region_ref[u] for u in range(units)]
    eye = (
        lax.broadcasted_iota(jnp.int32, (b, b), 0) == lax.broadcasted_iota(jnp.int32, (b, b), 1)
    ).astype(F32)
    own_first = HALO
    for u in range(own_units):
        for v in range(units):
            lo, hi = 0, 0
            for r, c, w in chunks:
                if r <= u + own_first < r + 2:
                    lo, hi = c, c + w
            if not lo <= v < hi:
                score_ref[lanes(u, 1), lanes(v, 1)] = jnp.zeros((b, b), F32)
    for r, c, w in chunks:
        scores = lax.dot_general(
            learned_ref[lanes(r, 2), :],
            swapped_ref[lanes(c, w), :],
            NT,
            preferred_element_type=F32,
        )
        for i in range(2):
            u = r + i
            mask = jnp.concatenate(
                [
                    jnp.full(
                        (1, b),
                        jnp.where((regions[u] == regions[v]) & (regions[u] >= 0), 1.0, 0.0),
                        F32,
                    )
                    for v in range(c, c + w)
                ],
                axis=1,
            )
            squashed = jnp.tanh(3.0 * scores[i * b : (i + 1) * b]) * mask
            if own_first <= u < own_first + own_units:
                score_ref[lanes(u - own_first, 1), lanes(c, w)] = squashed
            positive = jnp.maximum(squashed, 0.0)
            negative = jnp.minimum(squashed, 0.0)
            forward = positive * positive
            backward = negative * negative
            adj_ref[lanes(u, 1), : w * b] = forward.astype(BF16)
            adjt_ref[lanes(u, 1), : w * b] = backward.astype(BF16)
            own = lanes(u - c, 1)
            adj_ref[lanes(u, 1), own] = (forward[:, own] + eye).astype(BF16)
            adjt_ref[lanes(u, 1), own] = (backward[:, own] + eye).astype(BF16)
            degree = 1.0 + jnp.sum(forward, axis=1, keepdims=True)
            rdeg_ref[lanes(u, 1), :] = jnp.broadcast_to(1.0 / degree, (b, width))

    def twice(values):
        return jnp.concatenate([values, values], axis=1)

    def per_step(rows, weight, dims):
        return jnp.concatenate(
            [
                lax.dot_general(
                    rows[:, s * width : (s + 1) * width], weight, dims, preferred_element_type=F32
                )
                for s in range(2)
            ],
            axis=1,
        )

    keep = 1.0 - KEEP_INPUT
    for r, _, _ in chunks:
        rows = lanes(r, 2)
        back_two = per_step(g_ref[rows, :], mix_ref[2], NT)
        q_two_ref[rows, :] = (keep * back_two * twice(rdeg_ref[rows, :])).astype(BF16)
    for r, c, w in chunks:
        rows = lanes(r, 2)
        carried = jnp.dot(
            adjt_ref[rows, : w * b], q_two_ref[lanes(c, w), :], preferred_element_type=F32
        )
        back_one = per_step(g_ref[rows, :], mix_ref[1], NT) + carried
        grad_one = (keep * back_one * twice(rdeg_ref[rows, :])).astype(BF16)
        q_one_ref[rows, :] = grad_one
        prop = jnp.dot(
            adj_ref[rows, : w * b], x_ref[lanes(c, w), :], preferred_element_type=F32
        ) * twice(rdeg_ref[rows, :])
        one_ref[rows, :] = (KEEP_INPUT * x_ref[rows, :].astype(F32) + keep * prop).astype(BF16)
        off_ref[rows, :] = jnp.broadcast_to(
            jnp.sum(grad_one.astype(F32) * prop, axis=1, keepdims=True), (2 * b, width)
        )
    own_start = own_first * b
    for r, c, w in chunks:
        rows = lanes(r, 2)
        prop = jnp.dot(
            adj_ref[rows, : w * b], one_ref[lanes(c, w), :], preferred_element_type=F32
        ) * twice(rdeg_ref[rows, :])
        hop_two = (KEEP_INPUT * x_ref[rows, :].astype(F32) + keep * prop).astype(BF16)
        offset = off_ref[rows, :] + jnp.broadcast_to(
            jnp.sum(q_two_ref[rows, :].astype(F32) * prop, axis=1, keepdims=True), (2 * b, width)
        )
        off_ref[rows, :] = offset
        for i in range(2):
            u = r + i
            offrow_ref[:, lanes(u, 1)] = jnp.transpose(offset[i * b : (i + 1) * b])[:8]
            if own_first <= u < own_first + own_units:
                own = lanes(u, 1)
                hops = (x_ref[own, :], one_ref[own, :], hop_two[i * b : (i + 1) * b])
                mixed = per_step(hops[0], mix_ref[0], (((1,), (0,)), ((), ())))
                for k in (1, 2):
                    mixed = mixed + per_step(hops[k], mix_ref[k], (((1,), (0,)), ((), ())))
                for s in range(2):
                    flat_ref[pl.ds(2 * (u - own_first) * b + s, b, stride=2), :] = mixed[
                        :, s * width : (s + 1) * width
                    ]
                x_two = hops[2]
                adjt_ref[own, adjt_ref.shape[1] - row :] = x_two
    out_ref[...] = flat_ref[...].astype(BF16)

    own = slice(own_start, own_start + nodes)
    groups = sums_ref.shape[0]
    rows_v = nodes // groups
    weight_rows = []
    for hop in (
        x_ref[own, :],
        one_ref[own, :],
        adjt_ref[own, adjt_ref.shape[1] - row :],
    ):
        total = jnp.zeros((width, width), F32)
        for s in range(2):
            cut = slice(s * width, (s + 1) * width)
            total = total + lax.dot_general(
                hop[:, cut], g_ref[own, cut], TN, preferred_element_type=F32
            )
        weight_rows.append((total * norm_scale).astype(BF16))
    weight_rows.append(jnp.zeros((groups * rows_v - 3 * width, width), BF16))
    weights = jnp.concatenate(weight_rows, axis=0)
    for k in range(groups):
        sums_ref[k, rows_v:, :] = weights[k * rows_v : (k + 1) * rows_v]

    diagonal = block_diagonal(proj_ref[...])
    for k in range(own_units // 2):
        c, w = 2 * k, 2 * HALO + 2
        rows = lanes(own_first + 2 * k, 2)
        columns = lanes(c, w)
        inner = lax.dot_general(
            q_one_ref[rows, :], x_ref[columns, :], NT, preferred_element_type=F32
        ) + lax.dot_general(
            q_two_ref[rows, :], one_ref[columns, :], NT, preferred_element_type=F32
        )
        inner_t = lax.dot_general(
            x_ref[rows, :], q_one_ref[columns, :], NT, preferred_element_type=F32
        ) + lax.dot_general(
            one_ref[rows, :], q_two_ref[columns, :], NT, preferred_element_type=F32
        )
        local = slice(2 * k * b, (2 * k + 2) * b)
        squashed = score_ref[local, columns]
        offset = jnp.concatenate([off_ref[rows, :]] * w, axis=1)
        chosen = jnp.where(
            squashed > 0.0, inner - offset, inner_t - offrow_ref[0:1, columns]
        )
        pair = (6.0 * squashed * (1.0 - squashed * squashed) * chosen).astype(BF16)
        grad_m = jnp.dot(pair, swapped_ref[columns, :], preferred_element_type=F32)
        mine = m_ref[local, :]
        grad = lax.dot_general(
            3.0 * (1.0 - mine * mine) * grad_m,
            diagonal,
            NT,
            precision=HIGHEST,
            preferred_element_type=F32,
        ).astype(BF16)
        per = 2 * b // rows_v
        for j in range(per):
            sums_ref[k * per + j, :rows_v, :] = grad[j * rows_v : (j + 1) * rows_v]


def device_groups(counts, kept):
    strides = [math.prod(counts[i + 1 :]) for i in range(len(counts))]

    def spread(axes):
        numbers = [0]
        for i in axes:
            numbers = [n + k * strides[i] for n in numbers for k in range(counts[i])]
        return numbers

    others = [i for i in range(len(counts)) if i not in kept]
    return [[base + k for k in spread(kept)] for base in spread(others)]


def body(features, node_vectors, projections, mix_weight, region_sizes, cotangent):
    nodes, _, steps, width = features.shape
    axes = ("node", "win")
    node_count, win_count = lax.axis_size("node"), lax.axis_size("win")
    own_units = nodes // BLOCK
    units = own_units + 2 * HALO
    rim = HALO * BLOCK
    flat = nodes * steps
    head, tail, learned = pl.pallas_call(
        pack_kernel,
        name="pack",
        out_shape=(
            jax.ShapeDtypeStruct((rim, 5 * width), BF16),
            jax.ShapeDtypeStruct((rim, 5 * width), BF16),
            jax.ShapeDtypeStruct((nodes, width), F32),
        ),
        scratch_shapes=[pltpu.VMEM((flat, width), F32)],
        compiler_params=pltpu.CompilerParams(vmem_limit_bytes=16 << 20),
    )(
        features.reshape(flat, width),
        cotangent.reshape(flat, width),
        node_vectors,
        projections,
    )
    low = lax.ppermute(tail, "node", [(i, i + 1) for i in range(node_count - 1)])
    high = lax.ppermute(head, "node", [(i + 1, i) for i in range(node_count - 1)])
    unit = lax.axis_index("node") * own_units - HALO + jnp.arange(units, dtype=jnp.int32)
    ends = jnp.cumsum(region_sizes)
    region = jnp.sum((ends[None, :] <= unit[:, None]).astype(jnp.int32), axis=1)
    in_range = (unit >= 0) & (unit < node_count * own_units)
    region = jnp.where(in_range, region, -1)

    span = units * BLOCK
    y_count, x_count = 4, win_count
    inner_count = node_count // y_count
    groups = y_count * x_count
    rows_v = nodes // groups
    band = (2 * HALO + 2) * BLOCK
    row = steps * width
    out, sums = pl.pallas_call(
        partial(layer_kernel, 1.0 / math.sqrt(flat * node_count * win_count)),
        name="layer",
        in_specs=[pl.BlockSpec(memory_space=pltpu.SMEM)]
        + [pl.BlockSpec(memory_space=pltpu.VMEM)] * 7,
        out_shape=(
            jax.ShapeDtypeStruct((flat, width), BF16),
            jax.ShapeDtypeStruct((groups, 2 * rows_v, width), BF16),
        ),
        scratch_shapes=[
            pltpu.VMEM((span, row), BF16),
            pltpu.VMEM((span, row), BF16),
            pltpu.VMEM((span, width), BF16),
            pltpu.VMEM((span, width), BF16),
            pltpu.VMEM((span, band), BF16),
            pltpu.VMEM((span, band + row), BF16),
            pltpu.VMEM((nodes, span), F32),
            pltpu.VMEM((span, width), F32),
            pltpu.VMEM((span, row), BF16),
            pltpu.VMEM((span, row), BF16),
            pltpu.VMEM((span, row), BF16),
            pltpu.VMEM((span, width), F32),
            pltpu.VMEM((8, span), F32),
            pltpu.VMEM((flat, width), F32),
        ],
        compiler_params=pltpu.CompilerParams(vmem_limit_bytes=40 << 20),
    )(region, low, high, head, tail, learned, projections, mix_weight)

    counts = (y_count, inner_count, win_count)
    outer_groups = device_groups(counts, (0, 2))
    inner_groups = device_groups(counts, (1,))
    exchange = partial(
        lax.all_to_all, axis_name=axes, split_axis=0, concat_axis=0, tiled=True
    )
    got = exchange(sums, axis_index_groups=outer_groups).astype(F32)
    vector_sum = jnp.sum(
        got[:, :rows_v].reshape(y_count, win_count, rows_v, width), axis=1
    ).astype(BF16)
    weight_sum = jnp.sum(got[:, rows_v:], axis=0).astype(BF16)
    got = exchange(
        jnp.broadcast_to(weight_sum[None], (inner_count, rows_v, width)),
        axis_index_groups=inner_groups,
    ).astype(F32)
    weight_sum = jnp.sum(got, axis=0).astype(BF16)
    back = jnp.concatenate(
        [
            jnp.broadcast_to(
                vector_sum[:, None], (y_count, win_count, rows_v, width)
            ).reshape(groups, rows_v, width),
            jnp.broadcast_to(weight_sum[None], (groups, rows_v, width)),
        ],
        axis=1,
    )
    got = exchange(back, axis_index_groups=outer_groups).astype(F32)
    vector_grad = got[:, :rows_v].reshape(nodes, width)
    weight_grad = got[:, rows_v:].reshape(nodes, width)[: 3 * width].reshape(3, width, width)
    return (out.reshape(features.shape), vector_grad, weight_grad)


def solution(mesh):
    placed = (
        P("node", "win", None, None),
        P("node", None),
        P(),
        P(),
        P(),
        P("node", "win", None, None),
    )
    return jax.shard_map(
        body,
        mesh=mesh,
        in_specs=placed,
        out_specs=(P("node", "win", None, None), P("node", None), P()),
        check_vma=False,
    )
```

```python
from functools import partial
import math

import jax
import jax.numpy as jnp
from jax import lax
from jax.experimental import pallas as pl
from jax.experimental.pallas import tpu as pltpu
from jax.sharding import PartitionSpec as P

BLOCK = 128
HALO = 3
KEEP_INPUT = 0.05
F32 = jnp.float32
BF16 = jnp.bfloat16
NT = (((1,), (1,)), ((), ()))
TN = (((0,), (0,)), ((), ()))
HIGHEST = lax.Precision.HIGHEST


def block_diagonal(projections):
    zero = jnp.zeros_like(projections[0])
    return jnp.concatenate(
        [
            jnp.concatenate([projections[0], zero], axis=1),
            jnp.concatenate([zero, projections[1]], axis=1),
        ],
        axis=0,
    )


def pack_kernel(
    x_hbm, g_hbm, nv_hbm, proj_hbm, own_ref, far_ref, near_ref, m_ref, x_in, g_in, nv_in, proj_in,
    flat_ref, sems,
):
    copies = [
        pltpu.make_async_copy(source, target, sems.at[i])
        for i, (source, target) in enumerate(
            ((x_hbm, x_in), (g_hbm, g_in), (nv_hbm, nv_in), (proj_hbm, proj_in))
        )
    ]
    for copy in copies:
        copy.start()
    nodes, width = m_ref.shape
    rim = far_ref.shape[0]
    for part, source in enumerate((x_in, g_in)):
        copies[part].wait()
        flat_ref[...] = source[...].astype(F32)
        for step in range(2):
            rows = flat_ref[pl.ds(step, nodes, stride=2), :].astype(BF16)
            own_ref[:, (2 * part + step) * width : (2 * part + step + 1) * width] = rows
    copies[2].wait()
    copies[3].wait()
    learned = jnp.tanh(
        3.0
        * jnp.dot(
            nv_in[...],
            block_diagonal(proj_in[...]),
            precision=HIGHEST,
            preferred_element_type=F32,
        )
    )
    m_ref[...] = learned
    own_ref[:, 4 * width :] = learned.astype(BF16)
    odd = lax.rem(lax.axis_index("node"), 2)
    gap = nodes - rim
    far_ref[...] = own_ref[pl.ds(pl.multiple_of(odd * gap, BLOCK), rim), :]
    near_ref[...] = own_ref[pl.ds(pl.multiple_of((1 - odd) * gap, BLOCK), rim), :]


def layer_kernel(
    norm_scale,
    region_ref,
    first_ref,
    far_ref,
    near_ref,
    own_ref,
    m_ref,
    proj_ref,
    mix_ref,
    out_ref,
    sums_ref,
    x_ref,
    g_ref,
    learned_ref,
    swapped_ref,
    adj_ref,
    adjt_ref,
    score_ref,
    rdeg_ref,
    one_ref,
    two_ref,
    q_one_ref,
    q_two_ref,
    off_ref,
    offrow_ref,
    flat_ref,
):
    b = BLOCK
    nodes, width = m_ref.shape
    rim = far_ref.shape[0]
    own_units = nodes // b
    units = own_units + 2 * HALO
    reach = HALO + 1
    row = 2 * width
    odd = lax.rem(lax.axis_index("node"), 2)
    span = rim + nodes
    pieces = (
        (pl.multiple_of(odd * span, b), far_ref, rim),
        (rim, own_ref, nodes),
        (pl.multiple_of((1 - odd) * span, b), near_ref, rim),
    )
    for start, source, count in pieces:
        place = pl.ds(start, count)
        x_ref[place, :] = source[:, :row]
        g_ref[place, :] = source[:, row : 2 * row]
        learned_ref[place, :] = source[:, 2 * row :]
    learned = learned_ref[...]
    half = width // 2
    swapped_ref[...] = jnp.concatenate([learned[:, half:], -learned[:, :half]], axis=1)

    def unit_rows(first, count=1):
        return slice(first * b, (first + count) * b)

    firsts = [first_ref[u] for u in range(units)]
    windows = [pl.ds(pl.multiple_of(firsts[u] * b, b), reach * b) for u in range(units)]
    eye = (
        lax.broadcasted_iota(jnp.int32, (b, b), 0) == lax.broadcasted_iota(jnp.int32, (b, b), 1)
    ).astype(F32)
    own_first = HALO
    own_last = own_first + own_units
    for u in range(units):
        rows = unit_rows(u)
        scores = lax.dot_general(
            learned_ref[rows, :], swapped_ref[windows[u], :], NT, preferred_element_type=F32
        )
        mine = region_ref[u]
        mask = jnp.concatenate(
            [
                jnp.full(
                    (1, b),
                    jnp.where((region_ref[firsts[u] + k] == mine) & (mine >= 0), 1.0, 0.0),
                    F32,
                )
                for k in range(reach)
            ],
            axis=1,
        )
        squashed = jnp.tanh(3.0 * scores) * mask
        if own_first <= u < own_last:
            score_ref[unit_rows(u - own_first), :] = squashed
        positive = jnp.maximum(squashed, 0.0)
        negative = jnp.minimum(squashed, 0.0)
        forward = positive * positive
        adj_ref[rows, :] = forward.astype(BF16)
        adjt_ref[rows, :] = (negative * negative).astype(BF16)
        diagonal = pl.ds(pl.multiple_of((u - firsts[u]) * b, b), b)
        adj_ref[rows, diagonal] = (adj_ref[rows, diagonal].astype(F32) + eye).astype(BF16)
        adjt_ref[rows, diagonal] = (adjt_ref[rows, diagonal].astype(F32) + eye).astype(BF16)
        degree = 1.0 + jnp.sum(forward, axis=1, keepdims=True)
        rdeg_ref[rows, :] = jnp.broadcast_to(1.0 / degree, (b, width))

    def twice(values):
        return jnp.concatenate([values, values], axis=1)

    def per_step(rows, weight, dims):
        return jnp.concatenate(
            [
                lax.dot_general(
                    rows[:, s * width : (s + 1) * width], weight, dims, preferred_element_type=F32
                )
                for s in range(2)
            ],
            axis=1,
        )

    keep = 1.0 - KEEP_INPUT
    for r in range(0, units, 2):
        rows = unit_rows(r, 2)
        back_two = per_step(g_ref[rows, :], mix_ref[2], NT)
        q_two_ref[rows, :] = (keep * back_two * twice(rdeg_ref[rows, :])).astype(BF16)
    for u in range(units):
        rows = unit_rows(u)
        rdeg = twice(rdeg_ref[rows, :])
        carried = jnp.dot(
            adjt_ref[rows, :], q_two_ref[windows[u], :], preferred_element_type=F32
        )
        back_one = per_step(g_ref[rows, :], mix_ref[1], NT) + carried
        grad_one = (keep * back_one * rdeg).astype(BF16)
        q_one_ref[rows, :] = grad_one
        prop = jnp.dot(adj_ref[rows, :], x_ref[windows[u], :], preferred_element_type=F32) * rdeg
        one_ref[rows, :] = (KEEP_INPUT * x_ref[rows, :].astype(F32) + keep * prop).astype(BF16)
        off_ref[rows, :] = jnp.broadcast_to(
            jnp.sum(grad_one.astype(F32) * prop, axis=1, keepdims=True), (b, width)
        )
    for u in range(units):
        rows = unit_rows(u)
        prop = jnp.dot(
            adj_ref[rows, :], one_ref[windows[u], :], preferred_element_type=F32
        ) * twice(rdeg_ref[rows, :])
        offset = off_ref[rows, :] + jnp.broadcast_to(
            jnp.sum(q_two_ref[rows, :].astype(F32) * prop, axis=1, keepdims=True), (b, width)
        )
        off_ref[rows, :] = offset
        offrow_ref[u] = jnp.transpose(offset)[:8]
        if own_first <= u < own_last:
            two_ref[unit_rows(u - own_first), :] = (
                KEEP_INPUT * x_ref[rows, :].astype(F32) + keep * prop
            ).astype(BF16)

    own = unit_rows(own_first, own_units)
    hops = (x_ref[own, :], one_ref[own, :], two_ref[...])
    plain = (((1,), (0,)), ((), ()))
    mixed = per_step(hops[0], mix_ref[0], plain)
    for k in (1, 2):
        mixed = mixed + per_step(hops[k], mix_ref[k], plain)
    for s in range(2):
        flat_ref[pl.ds(s, nodes, stride=2), :] = mixed[:, s * width : (s + 1) * width]
    out_ref[...] = flat_ref[...].astype(BF16)

    groups = sums_ref.shape[0]
    rows_v = nodes // groups
    weight_rows = []
    for hop in hops:
        total = jnp.zeros((width, width), F32)
        for s in range(2):
            cut = slice(s * width, (s + 1) * width)
            total = total + lax.dot_general(
                hop[:, cut], g_ref[own, cut], TN, preferred_element_type=F32
            )
        weight_rows.append((total * norm_scale).astype(BF16))
    weight_rows.append(jnp.zeros((groups * rows_v - 3 * width, width), BF16))
    weights = jnp.concatenate(weight_rows, axis=0)
    for k in range(groups):
        sums_ref[k, rows_v:, :] = weights[k * rows_v : (k + 1) * rows_v]

    diagonal = block_diagonal(proj_ref[...])
    for u in range(own_first, own_last):
        rows = unit_rows(u)
        columns = windows[u]
        inner = lax.dot_general(
            q_one_ref[rows, :], x_ref[columns, :], NT, preferred_element_type=F32
        ) + lax.dot_general(
            q_two_ref[rows, :], one_ref[columns, :], NT, preferred_element_type=F32
        )
        inner_t = lax.dot_general(
            x_ref[rows, :], q_one_ref[columns, :], NT, preferred_element_type=F32
        ) + lax.dot_general(
            one_ref[rows, :], q_two_ref[columns, :], NT, preferred_element_type=F32
        )
        local = unit_rows(u - own_first)
        squashed = score_ref[local, :]
        offset = jnp.concatenate([off_ref[rows, :]] * reach, axis=1)
        offset_t = jnp.concatenate(
            [offrow_ref[firsts[u] + k, 0:1, :] for k in range(reach)], axis=1
        )
        chosen = jnp.where(squashed > 0.0, inner - offset, inner_t - offset_t)
        pair = (6.0 * squashed * (1.0 - squashed * squashed) * chosen).astype(BF16)
        grad_m = jnp.dot(pair, swapped_ref[columns, :], preferred_element_type=F32)
        mine = m_ref[local, :]
        grad = lax.dot_general(
            3.0 * (1.0 - mine * mine) * grad_m,
            diagonal,
            NT,
            precision=HIGHEST,
            preferred_element_type=F32,
        ).astype(BF16)
        per = b // rows_v
        for j in range(per):
            sums_ref[(u - own_first) * per + j, :rows_v, :] = grad[j * rows_v : (j + 1) * rows_v]


def finish_kernel(got_ref, vector_ref, weight_ref):
    groups, rows = got_ref.shape[:2]
    half = rows // 2
    for k in range(groups):
        got = got_ref[k].astype(F32)
        vector_ref[k * half : (k + 1) * half, :] = got[:half]
        if (k + 1) * half <= weight_ref.shape[0]:
            weight_ref[k * half : (k + 1) * half, :] = got[half:]


def device_groups(counts, kept):
    strides = [math.prod(counts[i + 1 :]) for i in range(len(counts))]

    def spread(axes):
        numbers = [0]
        for i in axes:
            numbers = [n + k * strides[i] for n in numbers for k in range(counts[i])]
        return numbers

    others = [i for i in range(len(counts)) if i not in kept]
    return [[base + k for k in spread(kept)] for base in spread(others)]


def body(features, node_vectors, projections, mix_weight, region_sizes, cotangent):
    nodes, _, steps, width = features.shape
    axes = ("node", "win")
    node_count, win_count = lax.axis_size("node"), lax.axis_size("win")
    own_units = nodes // BLOCK
    units = own_units + 2 * HALO
    rim = HALO * BLOCK
    flat = nodes * steps
    row = steps * width
    in_vmem = pl.BlockSpec(memory_space=pltpu.VMEM)
    in_hbm = pl.BlockSpec(memory_space=pltpu.HBM)
    own, far, near, learned = pl.pallas_call(
        pack_kernel,
        name="pack",
        in_specs=[in_hbm] * 4,
        out_shape=(
            jax.ShapeDtypeStruct((nodes, 5 * width), BF16),
            jax.ShapeDtypeStruct((rim, 5 * width), BF16),
            jax.ShapeDtypeStruct((rim, 5 * width), BF16),
            jax.ShapeDtypeStruct((nodes, width), F32),
        ),
        scratch_shapes=[
            pltpu.VMEM((flat, width), BF16),
            pltpu.VMEM((flat, width), BF16),
            pltpu.VMEM((nodes, width), F32),
            pltpu.VMEM(projections.shape, F32),
            pltpu.VMEM((flat, width), F32),
            pltpu.SemaphoreType.DMA((4,)),
        ],
        compiler_params=pltpu.CompilerParams(vmem_limit_bytes=16 << 20),
    )(
        features.reshape(flat, width),
        cotangent.reshape(flat, width),
        node_vectors,
        projections,
    )
    border = [(i, i + 1) for i in range(1, node_count - 1, 2)]
    inside = [(i, i + 1) for i in range(0, node_count, 2)]
    far = lax.ppermute(far, "node", border + [(j, i) for i, j in border])
    near = lax.ppermute(near, "node", inside + [(j, i) for i, j in inside])
    lead = lax.axis_index("node") * own_units - HALO
    place = jnp.arange(units, dtype=jnp.int32)
    unit = lead + place
    ends = jnp.cumsum(region_sizes)
    passed = (ends[None, :] <= unit[:, None]).astype(jnp.int32)
    in_range = (unit >= 0) & (unit < node_count * own_units)
    region = jnp.where(in_range, jnp.sum(passed, axis=1), -1)
    first = jnp.sum(passed * region_sizes[None, :], axis=1) - lead
    first = jnp.clip(
        first, jnp.maximum(place - HALO, 0), jnp.minimum(place, units - HALO - 1)
    )

    span = units * BLOCK
    y_count, x_count = 4, win_count
    inner_count = node_count // y_count
    groups = y_count * x_count
    rows_v = nodes // groups
    reach = (HALO + 1) * BLOCK
    out, sums = pl.pallas_call(
        partial(layer_kernel, 1.0 / math.sqrt(flat * node_count * win_count)),
        name="layer",
        in_specs=[pl.BlockSpec(memory_space=pltpu.SMEM)] * 2 + [in_vmem] * 6,
        out_shape=(
            jax.ShapeDtypeStruct((flat, width), BF16),
            jax.ShapeDtypeStruct((groups, 2 * rows_v, width), BF16),
        ),
        scratch_shapes=[
            pltpu.VMEM((span, row), BF16),
            pltpu.VMEM((span, row), BF16),
            pltpu.VMEM((span, width), BF16),
            pltpu.VMEM((span, width), BF16),
            pltpu.VMEM((span, reach), BF16),
            pltpu.VMEM((span, reach), BF16),
            pltpu.VMEM((nodes, reach), F32),
            pltpu.VMEM((span, width), F32),
            pltpu.VMEM((span, row), BF16),
            pltpu.VMEM((nodes, row), BF16),
            pltpu.VMEM((span, row), BF16),
            pltpu.VMEM((span, row), BF16),
            pltpu.VMEM((span, width), F32),
            pltpu.VMEM((units, 8, width), F32),
            pltpu.VMEM((flat, width), F32),
        ],
        compiler_params=pltpu.CompilerParams(vmem_limit_bytes=32 << 20),
    )(region, first, far, near, own, learned, projections, mix_weight)

    counts = (y_count, inner_count, win_count)
    outer_groups = device_groups(counts, (0, 2))
    inner_groups = device_groups(counts, (1,))
    exchange = partial(
        lax.all_to_all, axis_name=axes, split_axis=0, concat_axis=0, tiled=True
    )
    got = exchange(sums, axis_index_groups=outer_groups).astype(F32)
    vector_sum = jnp.sum(
        got[:, :rows_v].reshape(y_count, win_count, rows_v, width), axis=1
    ).astype(BF16)
    weight_sum = jnp.sum(got[:, rows_v:], axis=0).astype(BF16)
    got = exchange(
        jnp.broadcast_to(weight_sum[None], (inner_count, rows_v, width)),
        axis_index_groups=inner_groups,
    ).astype(F32)
    weight_sum = jnp.sum(got, axis=0).astype(BF16)
    back = jnp.concatenate(
        [
            jnp.broadcast_to(
                vector_sum[:, None], (y_count, win_count, rows_v, width)
            ).reshape(groups, rows_v, width),
            jnp.broadcast_to(weight_sum[None], (groups, rows_v, width)),
        ],
        axis=1,
    )
    got = exchange(back, axis_index_groups=outer_groups)
    vector_grad, weight_grad = pl.pallas_call(
        finish_kernel,
        name="finish",
        in_specs=[in_vmem],
        out_shape=(
            jax.ShapeDtypeStruct((nodes, width), F32),
            jax.ShapeDtypeStruct((3 * width, width), F32),
        ),
        compiler_params=pltpu.CompilerParams(vmem_limit_bytes=8 << 20),
    )(got)
    weight_grad = weight_grad.reshape(3, width, width)
    return (out.reshape(features.shape), vector_grad, weight_grad)


def solution(mesh):
    placed = (
        P("node", "win", None, None),
        P("node", None),
        P(),
        P(),
        P(),
        P("node", "win", None, None),
    )
    return jax.shard_map(
        body,
        mesh=mesh,
        in_specs=placed,
        out_specs=(P("node", "win", None, None), P("node", None), P()),
        check_vma=False,
    )
```

```python
from functools import partial
import math

import jax
import jax.numpy as jnp
from jax import lax
from jax.experimental import pallas as pl
from jax.experimental.pallas import tpu as pltpu
from jax.sharding import PartitionSpec as P

BLOCK = 128
HALO = 3
KEEP_INPUT = 0.05
F32 = jnp.float32
BF16 = jnp.bfloat16
NT = (((1,), (1,)), ((), ()))
TN = (((0,), (0,)), ((), ()))
HIGHEST = lax.Precision.HIGHEST


def block_diagonal(projections):
    zero = jnp.zeros_like(projections[0])
    return jnp.concatenate(
        [
            jnp.concatenate([projections[0], zero], axis=1),
            jnp.concatenate([zero, projections[1]], axis=1),
        ],
        axis=0,
    )


def pack_kernel(
    x_hbm, g_hbm, nv_hbm, proj_hbm, own_ref, far_ref, near_ref, m_ref, x_in, g_in, nv_in, proj_in,
    flat_ref, sems,
):
    copies = [
        pltpu.make_async_copy(source, target, sems.at[i])
        for i, (source, target) in enumerate(
            ((x_hbm, x_in), (g_hbm, g_in), (nv_hbm, nv_in), (proj_hbm, proj_in))
        )
    ]
    for copy in copies:
        copy.start()
    nodes, width = m_ref.shape
    rim = far_ref.shape[0]
    for part, source in enumerate((x_in, g_in)):
        copies[part].wait()
        flat_ref[...] = source[...].astype(F32)
        for step in range(2):
            rows = flat_ref[pl.ds(step, nodes, stride=2), :].astype(BF16)
            own_ref[:, (2 * part + step) * width : (2 * part + step + 1) * width] = rows
    copies[2].wait()
    copies[3].wait()
    learned = jnp.tanh(
        3.0
        * jnp.dot(
            nv_in[...],
            block_diagonal(proj_in[...]),
            precision=HIGHEST,
            preferred_element_type=F32,
        )
    )
    m_ref[...] = learned
    own_ref[:, 4 * width :] = learned.astype(BF16)
    odd = lax.rem(lax.axis_index("node"), 2)
    gap = nodes - rim
    far_ref[...] = own_ref[pl.ds(pl.multiple_of(odd * gap, BLOCK), rim), :]
    near_ref[...] = own_ref[pl.ds(pl.multiple_of((1 - odd) * gap, BLOCK), rim), :]


def layer_kernel(
    norm_scale,
    region_ref,
    first_ref,
    far_ref,
    near_ref,
    own_ref,
    m_ref,
    proj_ref,
    mix_ref,
    out_ref,
    sums_ref,
    x_ref,
    g_ref,
    learned_ref,
    swapped_ref,
    adj_ref,
    adjt_ref,
    score_ref,
    rdeg_ref,
    one_ref,
    two_ref,
    q_one_ref,
    q_two_ref,
    off_ref,
    offrow_ref,
    flat_ref,
):
    b = BLOCK
    nodes, width = m_ref.shape
    rim = far_ref.shape[0]
    own_units = nodes // b
    units = own_units + 2 * HALO
    reach = HALO + 1
    row = 2 * width
    odd = lax.rem(lax.axis_index("node"), 2)
    span = rim + nodes
    pieces = (
        (pl.multiple_of(odd * span, b), far_ref, rim),
        (rim, own_ref, nodes),
        (pl.multiple_of((1 - odd) * span, b), near_ref, rim),
    )
    for start, source, count in pieces:
        place = pl.ds(start, count)
        x_ref[place, :] = source[:, :row]
        g_ref[place, :] = source[:, row : 2 * row]
        learned_ref[place, :] = source[:, 2 * row :]
    learned = learned_ref[...]
    half = width // 2
    swapped_ref[...] = jnp.concatenate([learned[:, half:], -learned[:, :half]], axis=1)

    def unit_rows(first, count=1):
        return slice(first * b, (first + count) * b)

    firsts = [first_ref[u] for u in range(units)]
    windows = [pl.ds(pl.multiple_of(firsts[u] * b, b), reach * b) for u in range(units)]
    eye = (
        lax.broadcasted_iota(jnp.int32, (b, b), 0) == lax.broadcasted_iota(jnp.int32, (b, b), 1)
    ).astype(F32)
    own_first = HALO
    own_last = own_first + own_units
    for u in range(units):
        rows = unit_rows(u)
        scores = lax.dot_general(
            learned_ref[rows, :], swapped_ref[windows[u], :], NT, preferred_element_type=F32
        )
        mine = region_ref[u]
        mask = jnp.concatenate(
            [
                jnp.full(
                    (1, b),
                    jnp.where((region_ref[firsts[u] + k] == mine) & (mine >= 0), 1.0, 0.0),
                    F32,
                )
                for k in range(reach)
            ],
            axis=1,
        )
        squashed = jnp.tanh(3.0 * scores) * mask
        if own_first <= u < own_last:
            score_ref[unit_rows(u - own_first), :] = squashed
        positive = jnp.maximum(squashed, 0.0)
        negative = jnp.minimum(squashed, 0.0)
        forward = positive * positive
        adj_ref[rows, :] = forward.astype(BF16)
        adjt_ref[rows, :] = (negative * negative).astype(BF16)
        diagonal = pl.ds(pl.multiple_of((u - firsts[u]) * b, b), b)
        adj_ref[rows, diagonal] = (adj_ref[rows, diagonal].astype(F32) + eye).astype(BF16)
        adjt_ref[rows, diagonal] = (adjt_ref[rows, diagonal].astype(F32) + eye).astype(BF16)
        degree = 1.0 + jnp.sum(forward, axis=1, keepdims=True)
        rdeg_ref[rows, :] = jnp.broadcast_to(1.0 / degree, (b, width))

    def twice(values):
        return jnp.concatenate([values, values], axis=1)

    def per_step(rows, weight, dims):
        return jnp.concatenate(
            [
                lax.dot_general(
                    rows[:, s * width : (s + 1) * width], weight, dims, preferred_element_type=F32
                )
                for s in range(2)
            ],
            axis=1,
        )

    keep = 1.0 - KEEP_INPUT
    for r in range(0, units, 2):
        rows = unit_rows(r, 2)
        back_two = per_step(g_ref[rows, :], mix_ref[2], NT)
        q_two_ref[rows, :] = (keep * back_two * twice(rdeg_ref[rows, :])).astype(BF16)
    for u in range(units):
        rows = unit_rows(u)
        rdeg = twice(rdeg_ref[rows, :])
        carried = jnp.dot(
            adjt_ref[rows, :], q_two_ref[windows[u], :], preferred_element_type=F32
        )
        back_one = per_step(g_ref[rows, :], mix_ref[1], NT) + carried
        grad_one = (keep * back_one * rdeg).astype(BF16)
        q_one_ref[rows, :] = grad_one
        prop = jnp.dot(adj_ref[rows, :], x_ref[windows[u], :], preferred_element_type=F32) * rdeg
        one_ref[rows, :] = (KEEP_INPUT * x_ref[rows, :].astype(F32) + keep * prop).astype(BF16)
        off_ref[rows, :] = jnp.broadcast_to(
            jnp.sum(grad_one.astype(F32) * prop, axis=1, keepdims=True), (b, width)
        )
    for u in range(units):
        rows = unit_rows(u)
        prop = jnp.dot(
            adj_ref[rows, :], one_ref[windows[u], :], preferred_element_type=F32
        ) * twice(rdeg_ref[rows, :])
        offset = off_ref[rows, :] + jnp.broadcast_to(
            jnp.sum(q_two_ref[rows, :].astype(F32) * prop, axis=1, keepdims=True), (b, width)
        )
        off_ref[rows, :] = offset
        offrow_ref[u] = jnp.transpose(offset)[:8]
        if own_first <= u < own_last:
            two_ref[unit_rows(u - own_first), :] = (
                KEEP_INPUT * x_ref[rows, :].astype(F32) + keep * prop
            ).astype(BF16)

    own = unit_rows(own_first, own_units)
    hops = (x_ref[own, :], one_ref[own, :], two_ref[...])
    plain = (((1,), (0,)), ((), ()))
    mixed = per_step(hops[0], mix_ref[0], plain)
    for k in (1, 2):
        mixed = mixed + per_step(hops[k], mix_ref[k], plain)
    for s in range(2):
        flat_ref[pl.ds(s, nodes, stride=2), :] = mixed[:, s * width : (s + 1) * width]
    out_ref[...] = flat_ref[...].astype(BF16)

    groups = sums_ref.shape[0]
    rows_v = nodes // groups
    rows_w = 3 * width // groups
    weight_rows = []
    for hop in hops:
        total = jnp.zeros((width, width), F32)
        for s in range(2):
            cut = slice(s * width, (s + 1) * width)
            total = total + lax.dot_general(
                hop[:, cut], g_ref[own, cut], TN, preferred_element_type=F32
            )
        weight_rows.append(total * norm_scale)
    weights = jnp.concatenate(weight_rows, axis=0)
    for k in range(groups):
        sums_ref[k, rows_v:, :] = weights[k * rows_w : (k + 1) * rows_w].astype(BF16)

    diagonal = block_diagonal(proj_ref[...])
    for u in range(own_first, own_last):
        rows = unit_rows(u)
        columns = windows[u]
        inner = lax.dot_general(
            q_one_ref[rows, :], x_ref[columns, :], NT, preferred_element_type=F32
        ) + lax.dot_general(
            q_two_ref[rows, :], one_ref[columns, :], NT, preferred_element_type=F32
        )
        inner_t = lax.dot_general(
            x_ref[rows, :], q_one_ref[columns, :], NT, preferred_element_type=F32
        ) + lax.dot_general(
            one_ref[rows, :], q_two_ref[columns, :], NT, preferred_element_type=F32
        )
        local = unit_rows(u - own_first)
        squashed = score_ref[local, :]
        offset = jnp.concatenate([off_ref[rows, :]] * reach, axis=1)
        offset_t = jnp.concatenate(
            [offrow_ref[firsts[u] + k, 0:1, :] for k in range(reach)], axis=1
        )
        chosen = jnp.where(squashed > 0.0, inner - offset, inner_t - offset_t)
        pair = (6.0 * squashed * (1.0 - squashed * squashed) * chosen).astype(BF16)
        grad_m = jnp.dot(pair, swapped_ref[columns, :], preferred_element_type=F32)
        mine = m_ref[local, :]
        grad = lax.dot_general(
            3.0 * (1.0 - mine * mine) * grad_m,
            diagonal,
            NT,
            precision=HIGHEST,
            preferred_element_type=F32,
        ).astype(BF16)
        per = b // rows_v
        for j in range(per):
            sums_ref[(u - own_first) * per + j, :rows_v, :] = grad[j * rows_v : (j + 1) * rows_v]


def finish_kernel(got_ref, vector_ref, weight_ref):
    groups = got_ref.shape[0]
    rows_v = vector_ref.shape[0] // groups
    rows_w = weight_ref.shape[0] // groups
    for k in range(groups):
        got = got_ref[k].astype(F32)
        vector_ref[k * rows_v : (k + 1) * rows_v, :] = got[:rows_v]
        weight_ref[k * rows_w : (k + 1) * rows_w, :] = got[rows_v:]


def device_groups(counts, kept):
    strides = [math.prod(counts[i + 1 :]) for i in range(len(counts))]

    def spread(axes):
        numbers = [0]
        for i in axes:
            numbers = [n + k * strides[i] for n in numbers for k in range(counts[i])]
        return numbers

    others = [i for i in range(len(counts)) if i not in kept]
    return [[base + k for k in spread(kept)] for base in spread(others)]


def body(features, node_vectors, projections, mix_weight, region_sizes, cotangent):
    nodes, _, steps, width = features.shape
    axes = ("node", "win")
    node_count, win_count = lax.axis_size("node"), lax.axis_size("win")
    own_units = nodes // BLOCK
    units = own_units + 2 * HALO
    rim = HALO * BLOCK
    flat = nodes * steps
    row = steps * width
    in_vmem = pl.BlockSpec(memory_space=pltpu.VMEM)
    in_hbm = pl.BlockSpec(memory_space=pltpu.HBM)
    own, far, near, learned = pl.pallas_call(
        pack_kernel,
        name="pack",
        in_specs=[in_hbm] * 4,
        out_shape=(
            jax.ShapeDtypeStruct((nodes, 5 * width), BF16),
            jax.ShapeDtypeStruct((rim, 5 * width), BF16),
            jax.ShapeDtypeStruct((rim, 5 * width), BF16),
            jax.ShapeDtypeStruct((nodes, width), F32),
        ),
        scratch_shapes=[
            pltpu.VMEM((flat, width), BF16),
            pltpu.VMEM((flat, width), BF16),
            pltpu.VMEM((nodes, width), F32),
            pltpu.VMEM(projections.shape, F32),
            pltpu.VMEM((flat, width), F32),
            pltpu.SemaphoreType.DMA((4,)),
        ],
        compiler_params=pltpu.CompilerParams(vmem_limit_bytes=16 << 20),
    )(
        *(
            pltpu.with_memory_space_constraint(array, pltpu.HBM)
            for array in (
                features.reshape(flat, width),
                cotangent.reshape(flat, width),
                node_vectors,
                projections,
            )
        )
    )
    border = [(i, i + 1) for i in range(1, node_count - 1, 2)]
    inside = [(i, i + 1) for i in range(0, node_count, 2)]
    far = lax.ppermute(far, "node", border + [(j, i) for i, j in border])
    near = lax.ppermute(near, "node", inside + [(j, i) for i, j in inside])
    lead = lax.axis_index("node") * own_units - HALO
    place = jnp.arange(units, dtype=jnp.int32)
    unit = lead + place
    ends = jnp.cumsum(region_sizes)
    passed = (ends[None, :] <= unit[:, None]).astype(jnp.int32)
    in_range = (unit >= 0) & (unit < node_count * own_units)
    region = jnp.where(in_range, jnp.sum(passed, axis=1), -1)
    first = jnp.sum(passed * region_sizes[None, :], axis=1) - lead
    first = jnp.clip(
        first, jnp.maximum(place - HALO, 0), jnp.minimum(place, units - HALO - 1)
    )

    span = units * BLOCK
    y_far, y_near = 2, 2
    inner_count = node_count // (y_far * y_near)
    groups = y_far * win_count
    rows_v = nodes // groups
    rows_w = 3 * width // groups
    reach = (HALO + 1) * BLOCK
    out, sums = pl.pallas_call(
        partial(layer_kernel, 1.0 / math.sqrt(flat * node_count * win_count)),
        name="layer",
        in_specs=[pl.BlockSpec(memory_space=pltpu.SMEM)] * 2 + [in_vmem] * 6,
        out_shape=(
            jax.ShapeDtypeStruct((flat, width), BF16),
            jax.ShapeDtypeStruct((groups, rows_v + rows_w, width), BF16),
        ),
        scratch_shapes=[
            pltpu.VMEM((span, row), BF16),
            pltpu.VMEM((span, row), BF16),
            pltpu.VMEM((span, width), BF16),
            pltpu.VMEM((span, width), BF16),
            pltpu.VMEM((span, reach), BF16),
            pltpu.VMEM((span, reach), BF16),
            pltpu.VMEM((nodes, reach), F32),
            pltpu.VMEM((span, width), F32),
            pltpu.VMEM((span, row), BF16),
            pltpu.VMEM((nodes, row), BF16),
            pltpu.VMEM((span, row), BF16),
            pltpu.VMEM((span, row), BF16),
            pltpu.VMEM((span, width), F32),
            pltpu.VMEM((units, 8, width), F32),
            pltpu.VMEM((flat, width), F32),
        ],
        compiler_params=pltpu.CompilerParams(vmem_limit_bytes=32 << 20),
    )(region, first, far, near, own, learned, projections, mix_weight)

    counts = (y_far, y_near, inner_count, win_count)
    outer_groups = device_groups(counts, (0, 3))
    inner_groups = device_groups(counts, (1, 2))
    exchange = partial(
        lax.all_to_all, axis_name=axes, split_axis=0, concat_axis=0, tiled=True
    )
    got = exchange(sums, axis_index_groups=outer_groups).astype(F32)
    vector_sum = jnp.sum(
        got[:, :rows_v].reshape(y_far, win_count, rows_v, width), axis=1
    ).astype(BF16)
    weight_sum = jnp.sum(got[:, rows_v:], axis=0).astype(BF16)
    shares = jnp.broadcast_to(weight_sum[None], (y_near * inner_count, rows_w, width))
    vector_sum, shares = lax.optimization_barrier((vector_sum, shares))
    got = exchange(shares, axis_index_groups=inner_groups).astype(F32)
    weight_sum = jnp.sum(got, axis=0).astype(BF16)
    back = jnp.concatenate(
        [
            jnp.broadcast_to(
                vector_sum[:, None], (y_far, win_count, rows_v, width)
            ).reshape(groups, rows_v, width),
            jnp.broadcast_to(weight_sum[None], (groups, rows_w, width)),
        ],
        axis=1,
    )
    got = exchange(back, axis_index_groups=outer_groups)
    vector_grad, weight_grad = pl.pallas_call(
        finish_kernel,
        name="finish",
        in_specs=[in_vmem],
        out_shape=(
            jax.ShapeDtypeStruct((nodes, width), F32),
            jax.ShapeDtypeStruct((3 * width, width), F32),
        ),
        compiler_params=pltpu.CompilerParams(vmem_limit_bytes=8 << 20),
    )(got)
    weight_grad = weight_grad.reshape(3, width, width)
    return (out.reshape(features.shape), vector_grad, weight_grad)


def solution(mesh):
    placed = (
        P("node", "win", None, None),
        P("node", None),
        P(),
        P(),
        P(),
        P("node", "win", None, None),
    )
    return jax.shard_map(
        body,
        mesh=mesh,
        in_specs=placed,
        out_specs=(P("node", "win", None, None), P("node", None), P()),
        check_vma=False,
    )
```

```python
from functools import partial
import math

import jax
import jax.numpy as jnp
from jax import lax
from jax.experimental import pallas as pl
from jax.experimental.pallas import tpu as pltpu
from jax.sharding import PartitionSpec as P


BLOCK = 128
HALO = 3
KEEP_INPUT = 0.05
F32 = jnp.float32
BF16 = jnp.bfloat16
NT = (((1,), (1,)), ((), ()))
TN = (((0,), (0,)), ((), ()))
HIGHEST = lax.Precision.HIGHEST


def block_diagonal(projections):
    zero = jnp.zeros_like(projections[0])
    return jnp.concatenate(
        [
            jnp.concatenate([projections[0], zero], axis=1),
            jnp.concatenate([zero, projections[1]], axis=1),
        ],
        axis=0,
    )


def pack_kernel(
    x_hbm, g_hbm, nv_hbm, proj_hbm, own_ref, far_ref, far_g_ref, near_ref, m_ref, x_in, g_in, nv_in,
    proj_in, flat_ref, sems,
):
    copies = [
        pltpu.make_async_copy(source, target, sems.at[i])
        for i, (source, target) in enumerate(
            ((x_hbm, x_in), (g_hbm, g_in), (nv_hbm, nv_in), (proj_hbm, proj_in))
        )
    ]
    for copy in copies:
        copy.start()
    nodes, width = m_ref.shape
    rim = far_ref.shape[0]
    for part, source in enumerate((x_in, g_in)):
        copies[part].wait()
        flat_ref[...] = source[...].astype(F32)
        for step in range(2):
            rows = flat_ref[pl.ds(step, nodes, stride=2), :].astype(BF16)
            first = (1 + 2 * part + step) * width
            own_ref[:, first : first + width] = rows
    copies[2].wait()
    copies[3].wait()
    learned = jnp.tanh(
        3.0
        * jnp.dot(
            nv_in[...],
            block_diagonal(proj_in[...]),
            precision=HIGHEST,
            preferred_element_type=F32,
        )
    )
    m_ref[...] = learned
    own_ref[:, :width] = learned.astype(BF16)
    odd = lax.rem(lax.axis_index("node"), 2)
    gap = nodes - rim
    far_rows = pl.ds(pl.multiple_of(odd * gap, BLOCK), rim)
    far_ref[...] = own_ref[far_rows, : 3 * width]
    far_g_ref[...] = own_ref[far_rows, 3 * width :]
    near_ref[...] = own_ref[pl.ds(pl.multiple_of((1 - odd) * gap, BLOCK), rim), :]


def unit_rows(first, count=1):
    return slice(first * BLOCK, (first + count) * BLOCK)


def rim_places(rim, nodes):
    odd = lax.rem(lax.axis_index("node"), 2)
    span = rim + nodes
    return (
        pl.ds(pl.multiple_of(odd * span, BLOCK), rim),
        pl.ds(pl.multiple_of((1 - odd) * span, BLOCK), rim),
    )


def twice(values):
    return jnp.concatenate([values, values], axis=1)


def forward_kernel(
    norm_scale,
    region_ref,
    first_ref,
    far_ref,
    near_ref,
    own_ref,
    mix_hbm,
    out_ref,
    sums_ref,
    swapped_ref,
    hops_ref,
    props_ref,
    adjt_ref,
    score_ref,
    rdeg_ref,
    learned_ref,
    adj_ref,
    two_ref,
    flat_ref,
    mix_ref,
    sem,
):
    mix_copy = pltpu.make_async_copy(mix_hbm, mix_ref, sem)
    mix_copy.start()
    b = BLOCK
    nodes = own_ref.shape[0]
    rim, width = far_ref.shape[0], far_ref.shape[1] // 3
    own_units = nodes // b
    units = own_units + 2 * HALO
    reach = HALO + 1
    row = 2 * width
    half = width // 2
    far_place, near_place = rim_places(rim, nodes)
    own_place = pl.ds(rim, nodes)
    for place, source in ((far_place, far_ref), (own_place, own_ref), (near_place, near_ref)):
        learned = source[:, :width]
        learned_ref[place, :] = learned
        swapped_ref[place, :] = jnp.concatenate(
            [learned[:, half:], -learned[:, :half]], axis=1
        )
        hops_ref[place, :row] = source[:, width : 3 * width]

    firsts = [first_ref[u] for u in range(units)]
    eye = (
        lax.broadcasted_iota(jnp.int32, (b, b), 0) == lax.broadcasted_iota(jnp.int32, (b, b), 1)
    ).astype(F32)
    own_first = HALO
    own_last = own_first + own_units
    for u in range(units):
        rows = unit_rows(u)
        mine = region_ref[u]
        total = jnp.zeros((b, b), F32)
        for k in range(reach):
            other = firsts[u] + k
            scores = lax.dot_general(
                learned_ref[rows, :],
                swapped_ref[pl.ds(pl.multiple_of(other * b, b), b), :],
                NT,
                preferred_element_type=F32,
            )
            same = jnp.where((region_ref[other] == mine) & (mine >= 0), 1.0, 0.0)
            squashed = jnp.tanh(3.0 * scores) * same
            positive = jnp.maximum(squashed, 0.0)
            negative = jnp.minimum(squashed, 0.0)
            forward = positive * positive
            columns = unit_rows(k)
            if own_first <= u < own_last:
                score_ref[unit_rows(u - own_first), columns] = squashed
            adj_ref[rows, columns] = forward.astype(BF16)
            adjt_ref[rows, columns] = (negative * negative).astype(BF16)
            total = total + forward
        diagonal = pl.ds(pl.multiple_of((u - firsts[u]) * b, b), b)
        adj_ref[rows, diagonal] = (adj_ref[rows, diagonal].astype(F32) + eye).astype(BF16)
        adjt_ref[rows, diagonal] = (adjt_ref[rows, diagonal].astype(F32) + eye).astype(BF16)
        degree = 1.0 + jnp.sum(total, axis=1, keepdims=True)
        rdeg_ref[rows, :] = jnp.broadcast_to(1.0 / degree, (b, width))

    keep = 1.0 - KEEP_INPUT
    windows = [pl.ds(pl.multiple_of(firsts[u] * b, b), reach * b) for u in range(units)]
    for hop in range(2):
        source = slice(hop * row, (hop + 1) * row)
        for u in range(units):
            rows = unit_rows(u)
            prop = jnp.dot(
                adj_ref[rows, :], hops_ref[windows[u], source], preferred_element_type=F32
            ) * twice(rdeg_ref[rows, :])
            props_ref[rows, source] = prop.astype(BF16)
            if hop == 0:
                hops_ref[rows, row:] = (
                    KEEP_INPUT * hops_ref[rows, :row].astype(F32) + keep * prop
                ).astype(BF16)
            elif own_first <= u < own_last:
                two_ref[unit_rows(u - own_first), :] = (
                    KEEP_INPUT * hops_ref[rows, :row].astype(F32) + keep * prop
                ).astype(BF16)

    mix_copy.wait()
    weights = jnp.concatenate([mix_ref[0], mix_ref[1], mix_ref[2]], axis=0)
    all_hops, all_up = [], []
    for s in range(2):
        cut = slice(s * width, (s + 1) * width)
        all_hops.append(
            jnp.concatenate(
                [
                    hops_ref[own_place, cut],
                    hops_ref[own_place, row + s * width : row + (s + 1) * width],
                    two_ref[:, cut],
                ],
                axis=1,
            )
        )
        all_up.append(own_ref[:, 3 * width + s * width : 3 * width + (s + 1) * width])
        flat_ref[pl.ds(s, nodes, stride=2), :] = jnp.dot(
            all_hops[s], weights, preferred_element_type=F32
        )
    out_ref[...] = flat_ref[...].astype(BF16)
    sums_ref[...] = norm_scale * lax.dot_general(
        jnp.concatenate(all_hops, axis=0),
        jnp.concatenate(all_up, axis=0),
        TN,
        preferred_element_type=F32,
    )


def backward_kernel(
    first_ref,
    far_g_ref,
    near_ref,
    own_ref,
    m_ref,
    proj_hbm,
    mix_hbm,
    weight_ref,
    swapped_ref,
    hops_ref,
    props_ref,
    adjt_ref,
    score_ref,
    rdeg_ref,
    sums_ref,
    g_ref,
    q_ref,
    back_ref,
    off_ref,
    offrow_ref,
    dm_ref,
    mix_ref,
    proj_ref,
    sems,
):
    copies = (
        pltpu.make_async_copy(mix_hbm, mix_ref, sems.at[0]),
        pltpu.make_async_copy(proj_hbm, proj_ref, sems.at[1]),
    )
    for copy in copies:
        copy.start()
    b = BLOCK
    nodes, width = m_ref.shape
    rim = far_g_ref.shape[0]
    own_units = nodes // b
    units = own_units + 2 * HALO
    reach = HALO + 1
    row = 2 * width
    keep = 1.0 - KEEP_INPUT
    far_place, near_place = rim_places(rim, nodes)
    g_ref[far_place, :] = far_g_ref[...]
    g_ref[near_place, :] = near_ref[:, 3 * width :]
    g_ref[rim : rim + nodes, :] = own_ref[:, 3 * width :]
    firsts = [first_ref[u] for u in range(units)]
    windows = [pl.ds(pl.multiple_of(firsts[u] * b, b), reach * b) for u in range(units)]
    for copy in copies:
        copy.wait()
    mixed = jnp.concatenate([mix_ref[2], mix_ref[1]], axis=0)
    for r in range(0, units, 2):
        rows = unit_rows(r, 2)
        for s in range(2):
            cut = slice(s * width, (s + 1) * width)
            back = lax.dot_general(g_ref[rows, cut], mixed, NT, preferred_element_type=F32)
            q_ref[rows, row + s * width : row + (s + 1) * width] = (
                keep * back[:, :width] * rdeg_ref[rows, :]
            ).astype(BF16)
            back_ref[rows, cut] = back[:, width:]
    for u in range(units):
        rows = unit_rows(u)
        carried = jnp.dot(
            adjt_ref[rows, :], q_ref[windows[u], row:], preferred_element_type=F32
        )
        grad_one = (keep * (back_ref[rows, :] + carried) * twice(rdeg_ref[rows, :])).astype(BF16)
        q_ref[rows, :row] = grad_one
        inner = grad_one.astype(F32) * props_ref[rows, :row].astype(F32) + q_ref[
            rows, row:
        ].astype(F32) * props_ref[rows, row:].astype(F32)
        offset = jnp.broadcast_to(jnp.sum(inner, axis=1, keepdims=True), (b, width))
        off_ref[rows, :] = offset
        offrow_ref[u] = jnp.transpose(offset)[:8]

    own_first = HALO
    for u in range(own_first, own_first + own_units):
        rows = unit_rows(u)
        local = unit_rows(u - own_first)
        grad_m = jnp.zeros((b, width), F32)
        for k in range(0, reach, 2):
            columns = pl.ds(pl.multiple_of((firsts[u] + k) * b, b), 2 * b)
            inner = lax.dot_general(
                q_ref[rows, :], hops_ref[columns, :], NT, preferred_element_type=F32
            )
            inner_t = lax.dot_general(
                hops_ref[rows, :], q_ref[columns, :], NT, preferred_element_type=F32
            )
            squashed = score_ref[local, unit_rows(k, 2)]
            offset_t = jnp.concatenate(
                [offrow_ref[firsts[u] + k + i, 0:1, :] for i in range(2)], axis=1
            )
            chosen = jnp.where(
                squashed > 0.0, inner - twice(off_ref[rows, :]), inner_t - offset_t
            )
            pair = (6.0 * squashed * (1.0 - squashed * squashed) * chosen).astype(BF16)
            grad_m = grad_m + jnp.dot(
                pair, swapped_ref[columns, :], preferred_element_type=F32
            )
        mine = m_ref[local, :]
        dm_ref[local, :] = 3.0 * (1.0 - mine * mine) * grad_m
    grad = lax.dot_general(
        dm_ref[...],
        block_diagonal(proj_ref[...]),
        NT,
        precision=HIGHEST,
        preferred_element_type=F32,
    ).astype(BF16)
    groups = sums_ref.shape[0]
    rows_v = nodes // groups
    rows_w = weight_ref.shape[0] // groups
    for k in range(groups):
        sums_ref[k, :rows_v, :] = grad[k * rows_v : (k + 1) * rows_v]
        sums_ref[k, rows_v:, :] = weight_ref[k * rows_w : (k + 1) * rows_w].astype(BF16)


def finish_kernel(got_ref, vector_ref, weight_ref):
    groups = got_ref.shape[0]
    rows_v = vector_ref.shape[0] // groups
    rows_w = weight_ref.shape[0] // groups
    for k in range(groups):
        got = got_ref[k].astype(F32)
        vector_ref[k * rows_v : (k + 1) * rows_v, :] = got[:rows_v]
        weight_ref[k * rows_w : (k + 1) * rows_w, :] = got[rows_v:]


def device_groups(counts, kept):
    strides = [math.prod(counts[i + 1 :]) for i in range(len(counts))]

    def spread(axes):
        numbers = [0]
        for i in axes:
            numbers = [n + k * strides[i] for n in numbers for k in range(counts[i])]
        return numbers

    others = [i for i in range(len(counts)) if i not in kept]
    return [[base + k for k in spread(kept)] for base in spread(others)]


def body(features, node_vectors, projections, mix_weight, region_sizes, cotangent):
    nodes, _, steps, width = features.shape
    axes = ("node", "win")
    node_count, win_count = lax.axis_size("node"), lax.axis_size("win")
    own_units = nodes // BLOCK
    units = own_units + 2 * HALO
    rim = HALO * BLOCK
    flat = nodes * steps
    row = steps * width
    in_vmem = pl.BlockSpec(memory_space=pltpu.VMEM)
    in_hbm = pl.BlockSpec(memory_space=pltpu.HBM)
    features, cotangent = features.reshape(flat, width), cotangent.reshape(flat, width)
    features, cotangent, node_vectors, projections, mix_weight = (
        pltpu.with_memory_space_constraint(array, pltpu.HBM)
        for array in (features, cotangent, node_vectors, projections, mix_weight)
    )
    own, far, far_g, near, learned = pl.pallas_call(
        pack_kernel,
        name="pack",
        in_specs=[in_hbm] * 4,
        out_shape=(
            jax.ShapeDtypeStruct((nodes, 5 * width), BF16),
            jax.ShapeDtypeStruct((rim, 3 * width), BF16),
            jax.ShapeDtypeStruct((rim, 2 * width), BF16),
            jax.ShapeDtypeStruct((rim, 5 * width), BF16),
            jax.ShapeDtypeStruct((nodes, width), F32),
        ),
        scratch_shapes=[
            pltpu.VMEM((flat, width), BF16),
            pltpu.VMEM((flat, width), BF16),
            pltpu.VMEM((nodes, width), F32),
            pltpu.VMEM(projections.shape, F32),
            pltpu.VMEM((flat, width), F32),
            pltpu.SemaphoreType.DMA((4,)),
        ],
        compiler_params=pltpu.CompilerParams(vmem_limit_bytes=16 << 20),
    )(features, cotangent, node_vectors, projections)
    border = [(i, i + 1) for i in range(1, node_count - 1, 2)]
    inside = [(i, i + 1) for i in range(0, node_count, 2)]
    across = border + [(j, i) for i, j in border]
    far = lax.ppermute(far, "node", across)
    near = lax.ppermute(near, "node", inside + [(j, i) for i, j in inside])
    far_g = lax.ppermute(far_g, "node", across)
    lead = lax.axis_index("node") * own_units - HALO
    place = jnp.arange(units, dtype=jnp.int32)
    unit = lead + place
    ends = jnp.cumsum(region_sizes)
    passed = (ends[None, :] <= unit[:, None]).astype(jnp.int32)
    in_range = (unit >= 0) & (unit < node_count * own_units)
    region = jnp.where(in_range, jnp.sum(passed, axis=1), -1)
    first = jnp.sum(passed * region_sizes[None, :], axis=1) - lead
    first = jnp.clip(
        first, jnp.maximum(place - HALO, 0), jnp.minimum(place, units - HALO - 1)
    )

    span = units * BLOCK
    y_far, y_near = 2, 2
    inner_count = node_count // (y_far * y_near)
    groups = y_far * win_count
    rows_v = nodes // groups
    rows_w = 3 * width // groups
    reach = (HALO + 1) * BLOCK
    in_smem = pl.BlockSpec(memory_space=pltpu.SMEM)
    out, weights, *kept = pl.pallas_call(
        partial(forward_kernel, 1.0 / math.sqrt(flat * node_count * win_count)),
        name="forward",
        in_specs=[in_smem] * 2 + [in_vmem] * 3 + [in_hbm],
        out_shape=(
            jax.ShapeDtypeStruct((flat, width), BF16),
            jax.ShapeDtypeStruct((3 * width, width), F32),
            jax.ShapeDtypeStruct((span, width), BF16),
            jax.ShapeDtypeStruct((span, 2 * row), BF16),
            jax.ShapeDtypeStruct((span, 2 * row), BF16),
            jax.ShapeDtypeStruct((span, reach), BF16),
            jax.ShapeDtypeStruct((nodes, reach), F32),
            jax.ShapeDtypeStruct((span, width), F32),
        ),
        scratch_shapes=[
            pltpu.VMEM((span, width), BF16),
            pltpu.VMEM((span, reach), BF16),
            pltpu.VMEM((nodes, row), BF16),
            pltpu.VMEM((flat, width), F32),
            pltpu.VMEM(mix_weight.shape, BF16),
            pltpu.SemaphoreType.DMA,
        ],
        compiler_params=pltpu.CompilerParams(vmem_limit_bytes=24 << 20),
        cost_estimate=pl.CostEstimate(
            flops=6 * span * reach * row, bytes_accessed=8 << 20, transcendentals=span * reach
        ),
    )(region, first, far, near, own, mix_weight)
    sums = pl.pallas_call(
        backward_kernel,
        name="backward",
        in_specs=[in_smem] + [in_vmem] * 4 + [in_hbm] * 2 + [in_vmem] * 7,
        out_shape=jax.ShapeDtypeStruct((groups, rows_v + rows_w, width), BF16),
        scratch_shapes=[
            pltpu.VMEM((span, row), BF16),
            pltpu.VMEM((span, 2 * row), BF16),
            pltpu.VMEM((span, row), F32),
            pltpu.VMEM((span, width), F32),
            pltpu.VMEM((units, 8, width), F32),
            pltpu.VMEM((nodes, width), F32),
            pltpu.VMEM(mix_weight.shape, BF16),
            pltpu.VMEM(projections.shape, F32),
            pltpu.SemaphoreType.DMA((2,)),
        ],
        compiler_params=pltpu.CompilerParams(vmem_limit_bytes=24 << 20),
        cost_estimate=pl.CostEstimate(
            flops=6 * span * reach * row, bytes_accessed=8 << 20, transcendentals=0
        ),
    )(first, far_g, near, own, learned, projections, mix_weight, weights, *kept)

    counts = (y_far, y_near, inner_count, win_count)
    outer_groups = device_groups(counts, (0, 3))
    inner_groups = device_groups(counts, (1, 2))
    exchange = partial(
        lax.all_to_all, axis_name=axes, split_axis=0, concat_axis=0, tiled=True
    )
    got = exchange(sums, axis_index_groups=outer_groups).astype(F32)
    vector_sum = jnp.sum(
        got[:, :rows_v].reshape(y_far, win_count, rows_v, width), axis=1
    ).astype(BF16)
    weight_sum = jnp.sum(got[:, rows_v:], axis=0).astype(BF16)
    shares = jnp.broadcast_to(weight_sum[None], (y_near * inner_count, rows_w, width))
    vector_sum, shares = lax.optimization_barrier((vector_sum, shares))
    got = exchange(shares, axis_index_groups=inner_groups).astype(F32)
    weight_sum = jnp.sum(got, axis=0).astype(BF16)
    back = jnp.concatenate(
        [
            jnp.broadcast_to(
                vector_sum[:, None], (y_far, win_count, rows_v, width)
            ).reshape(groups, rows_v, width),
            jnp.broadcast_to(weight_sum[None], (groups, rows_w, width)),
        ],
        axis=1,
    )
    got = exchange(back, axis_index_groups=outer_groups)
    vector_grad, weight_grad = pl.pallas_call(
        finish_kernel,
        name="finish",
        in_specs=[in_vmem],
        out_shape=(
            jax.ShapeDtypeStruct((nodes, width), F32),
            jax.ShapeDtypeStruct((3 * width, width), F32),
        ),
        compiler_params=pltpu.CompilerParams(vmem_limit_bytes=8 << 20),
    )(got)
    weight_grad = weight_grad.reshape(3, width, width)
    return (out.reshape(nodes, 1, steps, width), vector_grad, weight_grad)


def solution(mesh):
    placed = (
        P("node", "win", None, None),
        P("node", None),
        P(),
        P(),
        P(),
        P("node", "win", None, None),
    )
    return jax.shard_map(
        body,
        mesh=mesh,
        in_specs=placed,
        out_specs=(P("node", "win", None, None), P("node", None), P()),
        check_vma=False,
    )
```

```python
from functools import partial
import math

import jax
import jax.numpy as jnp
from jax import lax
from jax.experimental import pallas as pl
from jax.experimental.pallas import tpu as pltpu
from jax.sharding import PartitionSpec as P


BLOCK = 128
HALO = 3
KEEP_INPUT = 0.05
F32 = jnp.float32
BF16 = jnp.bfloat16
NT = (((1,), (1,)), ((), ()))
TN = (((0,), (0,)), ((), ()))
HIGHEST = lax.Precision.HIGHEST


def block_diagonal(projections):
    zero = jnp.zeros_like(projections[0])
    return jnp.concatenate(
        [
            jnp.concatenate([projections[0], zero], axis=1),
            jnp.concatenate([zero, projections[1]], axis=1),
        ],
        axis=0,
    )


def pack_kernel(
    x_hbm, g_hbm, nv_hbm, proj_hbm, own_ref, far_ref, far_g_ref, near_ref, m_ref, x_in, g_in, nv_in,
    proj_in, flat_ref, sems,
):
    copies = [
        pltpu.make_async_copy(source, target, sems.at[i])
        for i, (source, target) in enumerate(
            ((x_hbm, x_in), (g_hbm, g_in), (nv_hbm, nv_in), (proj_hbm, proj_in))
        )
    ]
    for copy in copies:
        copy.start()
    nodes, width = m_ref.shape
    rim = far_ref.shape[0]
    for part, source in enumerate((x_in, g_in)):
        copies[part].wait()
        flat_ref[...] = source[...].astype(F32)
        for step in range(2):
            rows = flat_ref[pl.ds(step, nodes, stride=2), :].astype(BF16)
            first = (1 + 2 * part + step) * width
            own_ref[:, first : first + width] = rows
    copies[2].wait()
    copies[3].wait()
    learned = jnp.tanh(
        3.0
        * jnp.dot(
            nv_in[...],
            block_diagonal(proj_in[...]),
            precision=HIGHEST,
            preferred_element_type=F32,
        )
    )
    m_ref[...] = learned
    own_ref[:, :width] = learned.astype(BF16)
    odd = lax.rem(lax.axis_index("node"), 2)
    gap = nodes - rim
    far_rows = pl.ds(pl.multiple_of(odd * gap, BLOCK), rim)
    far_ref[...] = own_ref[far_rows, : 3 * width]
    far_g_ref[...] = own_ref[far_rows, 3 * width :]
    near_ref[...] = own_ref[pl.ds(pl.multiple_of((1 - odd) * gap, BLOCK), rim), :]


def unit_rows(first, count=1):
    return slice(first * BLOCK, (first + count) * BLOCK)


def rim_places(rim, nodes):
    odd = lax.rem(lax.axis_index("node"), 2)
    span = rim + nodes
    return (
        pl.ds(pl.multiple_of(odd * span, BLOCK), rim),
        pl.ds(pl.multiple_of((1 - odd) * span, BLOCK), rim),
    )


def beside(left, right):
    return jnp.concatenate([left, right], axis=1)


def twice(values):
    return beside(values, values)


def turned(learned):
    width = learned.shape[1]
    half = width // 2
    i = lax.broadcasted_iota(jnp.int32, (width, width), 0)
    j = lax.broadcasted_iota(jnp.int32, (width, width), 1)
    turn = jnp.where(i == j + half, 1.0, 0.0) - jnp.where(j == i + half, 1.0, 0.0)
    return jnp.dot(learned, turn.astype(BF16), preferred_element_type=F32).astype(BF16)


def forward_kernel(
    norm_scale,
    region_ref,
    first_ref,
    far_ref,
    near_ref,
    own_ref,
    mix_hbm,
    out_ref,
    sums_ref,
    swapped_ref,
    x_ref,
    one_ref,
    prop_one_ref,
    prop_two_ref,
    adjt_ref,
    score_ref,
    rdeg_ref,
    learned_ref,
    adj_ref,
    two_ref,
    flat_ref,
    mix_ref,
    sem,
):
    mix_copy = pltpu.make_async_copy(mix_hbm, mix_ref, sem)
    mix_copy.start()
    b = BLOCK
    nodes = own_ref.shape[0]
    rim, width = far_ref.shape[0], far_ref.shape[1] // 3
    own_units = nodes // b
    units = own_units + 2 * HALO
    reach = HALO + 1
    far_place, near_place = rim_places(rim, nodes)
    own_place = pl.ds(rim, nodes)
    for place, source in ((far_place, far_ref), (own_place, own_ref), (near_place, near_ref)):
        learned = source[:, :width]
        learned_ref[place, :] = learned
        swapped_ref[place, :] = turned(learned)
        x_ref[place, :] = source[:, width : 3 * width]

    firsts = [first_ref[u] for u in range(units)]
    eye = (
        lax.broadcasted_iota(jnp.int32, (b, b), 0) == lax.broadcasted_iota(jnp.int32, (b, b), 1)
    ).astype(F32)
    own_first = HALO
    own_last = own_first + own_units
    for u in range(units):
        rows = unit_rows(u)
        mine = region_ref[u]
        total = jnp.zeros((b, b), F32)
        for k in range(reach):
            other = firsts[u] + k
            scores = lax.dot_general(
                learned_ref[rows, :],
                swapped_ref[pl.ds(pl.multiple_of(other * b, b), b), :],
                NT,
                preferred_element_type=F32,
            )
            same = jnp.where((region_ref[other] == mine) & (mine >= 0), 3.0, 0.0)
            squashed = jnp.tanh(scores * same)
            positive = jnp.maximum(squashed, 0.0)
            negative = jnp.minimum(squashed, 0.0)
            forward = positive * positive
            columns = unit_rows(k)
            if own_first <= u < own_last:
                score_ref[unit_rows(u - own_first), columns] = squashed
            adj_ref[rows, columns] = forward.astype(BF16)
            adjt_ref[rows, columns] = (negative * negative).astype(BF16)
            total = total + forward
        degree = 1.0 + jnp.sum(total, axis=1, keepdims=True)
        rdeg_ref[rows, :] = jnp.broadcast_to(1.0 / degree, (b, width))
    for u in range(units):
        rows = unit_rows(u)
        diagonal = pl.ds(pl.multiple_of((u - firsts[u]) * b, b), b)
        adj_ref[rows, diagonal] = (adj_ref[rows, diagonal].astype(F32) + eye).astype(BF16)
        adjt_ref[rows, diagonal] = (adjt_ref[rows, diagonal].astype(F32) + eye).astype(BF16)

    keep = 1.0 - KEEP_INPUT
    windows = [pl.ds(pl.multiple_of(firsts[u] * b, b), reach * b) for u in range(units)]
    for u in range(units):
        rows = unit_rows(u)
        prop = jnp.dot(
            adj_ref[rows, :], x_ref[windows[u], :], preferred_element_type=F32
        ) * twice(rdeg_ref[rows, :])
        prop_one_ref[rows, :] = prop.astype(BF16)
        one_ref[rows, :] = (KEEP_INPUT * x_ref[rows, :].astype(F32) + keep * prop).astype(BF16)
    for u in range(units):
        rows = unit_rows(u)
        prop = jnp.dot(
            adj_ref[rows, :], one_ref[windows[u], :], preferred_element_type=F32
        ) * twice(rdeg_ref[rows, :])
        prop_two_ref[rows, :] = prop.astype(BF16)
        if own_first <= u < own_last:
            two_ref[unit_rows(u - own_first), :] = (
                KEEP_INPUT * x_ref[rows, :].astype(F32) + keep * prop
            ).astype(BF16)

    mix_copy.wait()
    weights = jnp.concatenate([mix_ref[0], mix_ref[1], mix_ref[2]], axis=0)
    all_hops, all_up = [], []
    for s in range(2):
        cut = slice(s * width, (s + 1) * width)
        all_hops.append(
            jnp.concatenate(
                [x_ref[own_place, cut], one_ref[own_place, cut], two_ref[:, cut]], axis=1
            )
        )
        all_up.append(own_ref[:, 3 * width + s * width : 3 * width + (s + 1) * width])
        flat_ref[pl.ds(s, nodes, stride=2), :] = jnp.dot(
            all_hops[s], weights, preferred_element_type=F32
        )
    out_ref[...] = flat_ref[...].astype(BF16)
    sums_ref[...] = norm_scale * lax.dot_general(
        jnp.concatenate(all_hops, axis=0),
        jnp.concatenate(all_up, axis=0),
        TN,
        preferred_element_type=F32,
    )


def backward_kernel(
    first_ref,
    far_g_ref,
    near_ref,
    own_ref,
    m_ref,
    proj_hbm,
    mix_hbm,
    weight_ref,
    swapped_ref,
    x_ref,
    one_ref,
    prop_one_ref,
    prop_two_ref,
    adjt_ref,
    score_ref,
    rdeg_ref,
    sums_ref,
    g_ref,
    q_one_ref,
    q_two_ref,
    back_ref,
    off_ref,
    offrow_ref,
    dm_ref,
    mix_ref,
    proj_ref,
    sems,
):
    copies = (
        pltpu.make_async_copy(mix_hbm, mix_ref, sems.at[0]),
        pltpu.make_async_copy(proj_hbm, proj_ref, sems.at[1]),
    )
    for copy in copies:
        copy.start()
    b = BLOCK
    nodes, width = m_ref.shape
    rim = far_g_ref.shape[0]
    own_units = nodes // b
    units = own_units + 2 * HALO
    reach = HALO + 1
    keep = 1.0 - KEEP_INPUT
    far_place, near_place = rim_places(rim, nodes)
    g_ref[far_place, :] = far_g_ref[...]
    g_ref[near_place, :] = near_ref[:, 3 * width :]
    g_ref[rim : rim + nodes, :] = own_ref[:, 3 * width :]
    firsts = [first_ref[u] for u in range(units)]
    windows = [pl.ds(pl.multiple_of(firsts[u] * b, b), reach * b) for u in range(units)]
    for copy in copies:
        copy.wait()
    mixed = jnp.concatenate([mix_ref[2], mix_ref[1]], axis=0)
    for r in range(0, units, 2):
        rows = unit_rows(r, 2)
        for s in range(2):
            cut = slice(s * width, (s + 1) * width)
            back = lax.dot_general(g_ref[rows, cut], mixed, NT, preferred_element_type=F32)
            q_two_ref[rows, cut] = (
                keep * back[:, :width] * rdeg_ref[rows, :]
            ).astype(BF16)
            back_ref[rows, cut] = back[:, width:]
    for u in range(units):
        rows = unit_rows(u)
        carried = jnp.dot(
            adjt_ref[rows, :], q_two_ref[windows[u], :], preferred_element_type=F32
        )
        grad_one = (keep * (back_ref[rows, :] + carried) * twice(rdeg_ref[rows, :])).astype(BF16)
        q_one_ref[rows, :] = grad_one
        inner = grad_one.astype(F32) * prop_one_ref[rows, :].astype(F32) + q_two_ref[
            rows, :
        ].astype(F32) * prop_two_ref[rows, :].astype(F32)
        offset = jnp.broadcast_to(jnp.sum(inner, axis=1, keepdims=True), (b, width))
        off_ref[rows, :] = offset
        offrow_ref[u] = jnp.transpose(offset)[:8]

    own_first = HALO
    for u in range(own_first, own_first + own_units):
        rows = unit_rows(u)
        local = unit_rows(u - own_first)
        grad_m = jnp.zeros((b, width), F32)
        for k in range(0, reach, 2):
            columns = pl.ds(pl.multiple_of((firsts[u] + k) * b, b), 2 * b)
            inner = lax.dot_general(
                beside(q_one_ref[rows, :], q_two_ref[rows, :]),
                beside(x_ref[columns, :], one_ref[columns, :]),
                NT,
                preferred_element_type=F32,
            )
            inner_t = lax.dot_general(
                beside(x_ref[rows, :], one_ref[rows, :]),
                beside(q_one_ref[columns, :], q_two_ref[columns, :]),
                NT,
                preferred_element_type=F32,
            )
            squashed = score_ref[local, unit_rows(k, 2)]
            offset_t = jnp.concatenate(
                [offrow_ref[firsts[u] + k + i, 0:1, :] for i in range(2)], axis=1
            )
            chosen = jnp.where(
                squashed > 0.0, inner - twice(off_ref[rows, :]), inner_t - offset_t
            )
            pair = (6.0 * squashed * (1.0 - squashed * squashed) * chosen).astype(BF16)
            grad_m = grad_m + jnp.dot(
                pair, swapped_ref[columns, :], preferred_element_type=F32
            )
        mine = m_ref[local, :]
        dm_ref[local, :] = 3.0 * (1.0 - mine * mine) * grad_m
    grad = lax.dot_general(
        dm_ref[...],
        block_diagonal(proj_ref[...]),
        NT,
        precision=HIGHEST,
        preferred_element_type=F32,
    ).astype(BF16)
    groups = sums_ref.shape[0]
    rows_v = nodes // groups
    rows_w = weight_ref.shape[0] // groups
    for k in range(groups):
        sums_ref[k, :rows_v, :] = grad[k * rows_v : (k + 1) * rows_v]
        sums_ref[k, rows_v:, :] = weight_ref[k * rows_w : (k + 1) * rows_w].astype(BF16)


def finish_kernel(got_ref, vector_ref, weight_ref):
    groups = got_ref.shape[0]
    rows_v = vector_ref.shape[0] // groups
    rows_w = weight_ref.shape[0] // groups
    for k in range(groups):
        got = got_ref[k].astype(F32)
        vector_ref[k * rows_v : (k + 1) * rows_v, :] = got[:rows_v]
        weight_ref[k * rows_w : (k + 1) * rows_w, :] = got[rows_v:]


def device_groups(counts, kept):
    strides = [math.prod(counts[i + 1 :]) for i in range(len(counts))]

    def spread(axes):
        numbers = [0]
        for i in axes:
            numbers = [n + k * strides[i] for n in numbers for k in range(counts[i])]
        return numbers

    others = [i for i in range(len(counts)) if i not in kept]
    return [[base + k for k in spread(kept)] for base in spread(others)]


def body(features, node_vectors, projections, mix_weight, region_sizes, cotangent):
    nodes, _, steps, width = features.shape
    axes = ("node", "win")
    node_count, win_count = lax.axis_size("node"), lax.axis_size("win")
    own_units = nodes // BLOCK
    units = own_units + 2 * HALO
    rim = HALO * BLOCK
    flat = nodes * steps
    row = steps * width
    in_vmem = pl.BlockSpec(memory_space=pltpu.VMEM)
    in_hbm = pl.BlockSpec(memory_space=pltpu.HBM)
    features, cotangent = features.reshape(flat, width), cotangent.reshape(flat, width)
    features, cotangent, node_vectors, projections, mix_weight = (
        pltpu.with_memory_space_constraint(array, pltpu.HBM)
        for array in (features, cotangent, node_vectors, projections, mix_weight)
    )
    own, far, far_g, near, learned = pl.pallas_call(
        pack_kernel,
        name="pack",
        in_specs=[in_hbm] * 4,
        out_shape=(
            jax.ShapeDtypeStruct((nodes, 5 * width), BF16),
            jax.ShapeDtypeStruct((rim, 3 * width), BF16),
            jax.ShapeDtypeStruct((rim, 2 * width), BF16),
            jax.ShapeDtypeStruct((rim, 5 * width), BF16),
            jax.ShapeDtypeStruct((nodes, width), F32),
        ),
        scratch_shapes=[
            pltpu.VMEM((flat, width), BF16),
            pltpu.VMEM((flat, width), BF16),
            pltpu.VMEM((nodes, width), F32),
            pltpu.VMEM(projections.shape, F32),
            pltpu.VMEM((flat, width), F32),
            pltpu.SemaphoreType.DMA((4,)),
        ],
        compiler_params=pltpu.CompilerParams(vmem_limit_bytes=16 << 20),
    )(features, cotangent, node_vectors, projections)
    border = [(i, i + 1) for i in range(1, node_count - 1, 2)]
    inside = [(i, i + 1) for i in range(0, node_count, 2)]
    across = border + [(j, i) for i, j in border]
    far = lax.ppermute(far, "node", across)
    near = lax.ppermute(near, "node", inside + [(j, i) for i, j in inside])
    far_g = lax.ppermute(far_g, "node", across)
    lead = lax.axis_index("node") * own_units - HALO
    place = jnp.arange(units, dtype=jnp.int32)
    unit = lead + place
    ends = jnp.cumsum(region_sizes)
    passed = (ends[None, :] <= unit[:, None]).astype(jnp.int32)
    in_range = (unit >= 0) & (unit < node_count * own_units)
    region = jnp.where(in_range, jnp.sum(passed, axis=1), -1)
    first = jnp.sum(passed * region_sizes[None, :], axis=1) - lead
    first = jnp.clip(first, jnp.maximum(place - HALO, 0), jnp.minimum(place, units - HALO - 1))

    span = units * BLOCK
    y_far, y_near = 2, 2
    inner_count = node_count // (y_far * y_near)
    groups = y_far * win_count
    rows_v = nodes // groups
    rows_w = 3 * width // groups
    reach = (HALO + 1) * BLOCK
    in_smem = pl.BlockSpec(memory_space=pltpu.SMEM)
    out, weights, *kept = pl.pallas_call(
        partial(forward_kernel, 1.0 / math.sqrt(flat * node_count * win_count)),
        name="forward",
        in_specs=[in_smem] * 2 + [in_vmem] * 3 + [in_hbm],
        out_shape=(
            jax.ShapeDtypeStruct((flat, width), BF16),
            jax.ShapeDtypeStruct((3 * width, width), F32),
            jax.ShapeDtypeStruct((span, width), BF16),
            jax.ShapeDtypeStruct((span, row), BF16),
            jax.ShapeDtypeStruct((span, row), BF16),
            jax.ShapeDtypeStruct((span, row), BF16),
            jax.ShapeDtypeStruct((span, row), BF16),
            jax.ShapeDtypeStruct((span, reach), BF16),
            jax.ShapeDtypeStruct((nodes, reach), F32),
            jax.ShapeDtypeStruct((span, width), F32),
        ),
        scratch_shapes=[
            pltpu.VMEM((span, width), BF16),
            pltpu.VMEM((span, reach), BF16),
            pltpu.VMEM((nodes, row), BF16),
            pltpu.VMEM((flat, width), F32),
            pltpu.VMEM(mix_weight.shape, BF16),
            pltpu.SemaphoreType.DMA,
        ],
        compiler_params=pltpu.CompilerParams(vmem_limit_bytes=24 << 20),
        cost_estimate=pl.CostEstimate(
            flops=6 * span * reach * row, bytes_accessed=8 << 20, transcendentals=span * reach
        ),
    )(region, first, far, near, own, mix_weight)
    sums = pl.pallas_call(
        backward_kernel,
        name="backward",
        in_specs=[in_smem] + [in_vmem] * 4 + [in_hbm] * 2 + [in_vmem] * 9,
        out_shape=jax.ShapeDtypeStruct((groups, rows_v + rows_w, width), BF16),
        scratch_shapes=[
            pltpu.VMEM((span, row), BF16),
            pltpu.VMEM((span, row), BF16),
            pltpu.VMEM((span, row), BF16),
            pltpu.VMEM((span, row), F32),
            pltpu.VMEM((span, width), F32),
            pltpu.VMEM((units, 8, width), F32),
            pltpu.VMEM((nodes, width), F32),
            pltpu.VMEM(mix_weight.shape, BF16),
            pltpu.VMEM(projections.shape, F32),
            pltpu.SemaphoreType.DMA((2,)),
        ],
        compiler_params=pltpu.CompilerParams(vmem_limit_bytes=24 << 20),
        cost_estimate=pl.CostEstimate(
            flops=6 * span * reach * row, bytes_accessed=8 << 20, transcendentals=0
        ),
    )(first, far_g, near, own, learned, projections, mix_weight, weights, *kept)

    counts = (y_far, y_near, inner_count, win_count)
    outer_groups = device_groups(counts, (0, 3))
    inner_groups = device_groups(counts, (1, 2))
    exchange = partial(
        lax.all_to_all, axis_name=axes, split_axis=0, concat_axis=0, tiled=True
    )
    got = exchange(sums, axis_index_groups=outer_groups).astype(F32)
    vector_sum = jnp.sum(
        got[:, :rows_v].reshape(y_far, win_count, rows_v, width), axis=1
    ).astype(BF16)
    weight_sum = jnp.sum(got[:, rows_v:], axis=0).astype(BF16)
    shares = jnp.broadcast_to(weight_sum[None], (y_near * inner_count, rows_w, width))
    vector_sum, shares = lax.optimization_barrier((vector_sum, shares))
    got = exchange(shares, axis_index_groups=inner_groups).astype(F32)
    weight_sum = jnp.sum(got, axis=0).astype(BF16)
    back = jnp.concatenate(
        [
            jnp.broadcast_to(
                vector_sum[:, None], (y_far, win_count, rows_v, width)
            ).reshape(groups, rows_v, width),
            jnp.broadcast_to(weight_sum[None], (groups, rows_w, width)),
        ],
        axis=1,
    )
    got = exchange(back, axis_index_groups=outer_groups)
    vector_grad, weight_grad = pl.pallas_call(
        finish_kernel,
        name="finish",
        in_specs=[in_vmem],
        out_shape=(
            jax.ShapeDtypeStruct((nodes, width), F32),
            jax.ShapeDtypeStruct((3 * width, width), F32),
        ),
        compiler_params=pltpu.CompilerParams(vmem_limit_bytes=8 << 20),
    )(got)
    weight_grad = weight_grad.reshape(3, width, width)
    return (out.reshape(nodes, 1, steps, width), vector_grad, weight_grad)


def solution(mesh):
    placed = (
        P("node", "win", None, None),
        P("node", None),
        P(),
        P(),
        P(),
        P("node", "win", None, None),
    )
    return jax.shard_map(
        body,
        mesh=mesh,
        in_specs=placed,
        out_specs=(P("node", "win", None, None), P("node", None), P()),
        check_vma=False,
    )
```

```python
from functools import partial
import math

import jax
import jax.numpy as jnp
from jax import lax
from jax.experimental import pallas as pl
from jax.experimental.pallas import tpu as pltpu
from jax.sharding import PartitionSpec as P


BLOCK = 128
HALO = 3
KEEP_INPUT = 0.05
F32 = jnp.float32
BF16 = jnp.bfloat16
NT = (((1,), (1,)), ((), ()))
TN = (((0,), (0,)), ((), ()))
HIGHEST = lax.Precision.HIGHEST


def block_diagonal(projections):
    zero = jnp.zeros_like(projections[0])
    return jnp.concatenate(
        [
            jnp.concatenate([projections[0], zero], axis=1),
            jnp.concatenate([zero, projections[1]], axis=1),
        ],
        axis=0,
    )


def pack_kernel(
    x_hbm, g_hbm, nv_hbm, proj_hbm, mix_hbm, own_ref, far_ref, near_ref, m_ref, proj_ref, mix_ref,
    x_in, g_in, nv_in, flat_ref, sems,
):
    copies = [
        pltpu.make_async_copy(source, target, sems.at[i])
        for i, (source, target) in enumerate(
            (
                (x_hbm, x_in),
                (g_hbm, g_in),
                (nv_hbm, nv_in),
                (proj_hbm, proj_ref),
                (mix_hbm, mix_ref),
            )
        )
    ]
    for copy in copies:
        copy.start()
    nodes, width = m_ref.shape
    rim = far_ref.shape[0]
    for part, source in enumerate((x_in, g_in)):
        copies[part].wait()
        flat_ref[...] = source[...].astype(F32)
        for step in range(2):
            rows = flat_ref[pl.ds(step, nodes, stride=2), :].astype(BF16)
            first = (1 + 2 * part + step) * width
            own_ref[:, first : first + width] = rows
    copies[2].wait()
    copies[3].wait()
    learned = jnp.tanh(
        3.0
        * jnp.dot(
            nv_in[...],
            block_diagonal(proj_ref[...]),
            precision=HIGHEST,
            preferred_element_type=F32,
        )
    )
    m_ref[...] = learned
    own_ref[:, :width] = learned.astype(BF16)
    odd = lax.rem(lax.axis_index("node"), 2)
    gap = nodes - rim
    far_ref[...] = own_ref[pl.ds(pl.multiple_of(odd * gap, BLOCK), rim), :]
    near_ref[...] = own_ref[pl.ds(pl.multiple_of((1 - odd) * gap, BLOCK), rim), :]
    copies[4].wait()


def unit_rows(first, count=1):
    return slice(first * BLOCK, (first + count) * BLOCK)


def rim_places(rim, nodes):
    odd = lax.rem(lax.axis_index("node"), 2)
    span = rim + nodes
    return (
        pl.ds(pl.multiple_of(odd * span, BLOCK), rim),
        pl.ds(pl.multiple_of((1 - odd) * span, BLOCK), rim),
    )


def beside(left, right):
    return jnp.concatenate([left, right], axis=1)


def twice(values):
    return beside(values, values)


def turned(learned):
    width = learned.shape[1]
    half = width // 2
    i = lax.broadcasted_iota(jnp.int32, (width, width), 0)
    j = lax.broadcasted_iota(jnp.int32, (width, width), 1)
    turn = jnp.where(i == j + half, 1.0, 0.0) - jnp.where(j == i + half, 1.0, 0.0)
    return jnp.dot(learned, turn.astype(BF16), preferred_element_type=F32).astype(BF16)


def layer_kernel(
    norm_scale,
    region_ref,
    first_ref,
    far_ref,
    near_ref,
    own_ref,
    m_ref,
    proj_ref,
    mix_ref,
    out_hbm,
    sums_ref,
    x_ref,
    g_ref,
    learned_ref,
    swapped_ref,
    adj_ref,
    adjt_ref,
    score_ref,
    rdeg_ref,
    one_ref,
    two_ref,
    q_one_ref,
    q_two_ref,
    back_ref,
    off_ref,
    offrow_ref,
    dm_ref,
    flat_ref,
    out_ref,
    sem,
):
    b = BLOCK
    nodes = own_ref.shape[0]
    rim, width = far_ref.shape[0], m_ref.shape[1]
    own_units = nodes // b
    units = own_units + 2 * HALO
    reach = HALO + 1
    row = 2 * width
    keep = 1.0 - KEEP_INPUT
    far_place, near_place = rim_places(rim, nodes)
    own_place = pl.ds(rim, nodes)
    for place, source in ((far_place, far_ref), (own_place, own_ref), (near_place, near_ref)):
        learned = source[:, :width]
        learned_ref[place, :] = learned
        swapped_ref[place, :] = turned(learned)
        x_ref[place, :] = source[:, width : width + row]
        g_ref[place, :] = source[:, width + row :]

    firsts = [first_ref[u] for u in range(units)]
    windows = [pl.ds(pl.multiple_of(firsts[u] * b, b), reach * b) for u in range(units)]
    eye = (
        lax.broadcasted_iota(jnp.int32, (b, b), 0) == lax.broadcasted_iota(jnp.int32, (b, b), 1)
    ).astype(F32)
    own_first = HALO
    own_last = own_first + own_units
    mixed = jnp.concatenate([mix_ref[2], mix_ref[1]], axis=0)
    for u in range(units):
        rows = unit_rows(u)
        mine = region_ref[u]
        total = jnp.zeros((b, b), F32)
        for k in range(reach):
            other = firsts[u] + k
            scores = lax.dot_general(
                learned_ref[rows, :],
                swapped_ref[pl.ds(pl.multiple_of(other * b, b), b), :],
                NT,
                preferred_element_type=F32,
            )
            same = jnp.where((region_ref[other] == mine) & (mine >= 0), 3.0, 0.0)
            squashed = jnp.tanh(scores * same)
            positive = jnp.maximum(squashed, 0.0)
            negative = jnp.minimum(squashed, 0.0)
            forward = positive * positive
            columns = unit_rows(k)
            if own_first <= u < own_last:
                score_ref[unit_rows(u - own_first), columns] = squashed
            adj_ref[rows, columns] = forward.astype(BF16)
            adjt_ref[rows, columns] = (negative * negative).astype(BF16)
            total = total + forward
        degree = 1.0 + jnp.sum(total, axis=1, keepdims=True)
        rdeg = jnp.broadcast_to(1.0 / degree, (b, width))
        rdeg_ref[rows, :] = rdeg
        for s in range(2):
            cut = slice(s * width, (s + 1) * width)
            back = lax.dot_general(g_ref[rows, cut], mixed, NT, preferred_element_type=F32)
            q_two_ref[rows, cut] = (keep * back[:, :width] * rdeg).astype(BF16)
            back_ref[rows, cut] = back[:, width:]
    for u in range(units):
        rows = unit_rows(u)
        diagonal = pl.ds(pl.multiple_of((u - firsts[u]) * b, b), b)
        adj_ref[rows, diagonal] = (adj_ref[rows, diagonal].astype(F32) + eye).astype(BF16)
        adjt_ref[rows, diagonal] = (adjt_ref[rows, diagonal].astype(F32) + eye).astype(BF16)

    order = list(range(own_first, own_last))
    order += [u for u in range(units) if u not in order]
    for u in order:
        rows = unit_rows(u)
        rdeg = twice(rdeg_ref[rows, :])
        carried = jnp.dot(
            adjt_ref[rows, :], q_two_ref[windows[u], :], preferred_element_type=F32
        )
        prop = jnp.dot(adj_ref[rows, :], x_ref[windows[u], :], preferred_element_type=F32) * rdeg
        one_ref[rows, :] = (KEEP_INPUT * x_ref[rows, :].astype(F32) + keep * prop).astype(BF16)
        grad_one = (keep * (back_ref[rows, :] + carried) * rdeg).astype(BF16)
        q_one_ref[rows, :] = grad_one
        inner = grad_one.astype(F32) * prop
        off_ref[rows, :] = inner[:, :width] + inner[:, width:]

    def second_hop(u):
        rows = unit_rows(u)
        prop = jnp.dot(
            adj_ref[rows, :], one_ref[windows[u], :], preferred_element_type=F32
        ) * twice(rdeg_ref[rows, :])
        inner = q_two_ref[rows, :].astype(F32) * prop
        inner = off_ref[rows, :] + inner[:, :width] + inner[:, width:]
        offset = jnp.broadcast_to(jnp.sum(inner, axis=1, keepdims=True), (b, width))
        off_ref[rows, :] = offset
        offrow_ref[u] = jnp.transpose(offset)[:8]
        if own_first <= u < own_last:
            two_ref[unit_rows(u - own_first), :] = (
                KEEP_INPUT * x_ref[rows, :].astype(F32) + keep * prop
            ).astype(BF16)

    for u in range(own_first, own_last):
        second_hop(u)
    weights = jnp.concatenate([mix_ref[0], mix_ref[1], mix_ref[2]], axis=0)
    all_hops, all_up = [], []
    for s in range(2):
        cut = slice(s * width, (s + 1) * width)
        all_hops.append(
            jnp.concatenate(
                [x_ref[own_place, cut], one_ref[own_place, cut], two_ref[:, cut]], axis=1
            )
        )
        all_up.append(g_ref[own_place, cut])
        flat_ref[pl.ds(s, nodes, stride=2), :] = jnp.dot(
            all_hops[s], weights, preferred_element_type=F32
        )
    out_ref[...] = flat_ref[...].astype(BF16)
    out_copy = pltpu.make_async_copy(out_ref, out_hbm, sem)
    out_copy.start()
    for u in range(units):
        if not own_first <= u < own_last:
            second_hop(u)
    groups = sums_ref.shape[0]
    rows_v = nodes // groups
    rows_w = 3 * width // groups
    weight = norm_scale * lax.dot_general(
        jnp.concatenate(all_hops, axis=0),
        jnp.concatenate(all_up, axis=0),
        TN,
        preferred_element_type=F32,
    )
    for k in range(groups):
        sums_ref[k, rows_v:, :] = weight[k * rows_w : (k + 1) * rows_w].astype(BF16)

    for u in range(own_first, own_last):
        rows = unit_rows(u)
        local = unit_rows(u - own_first)
        grad_m = jnp.zeros((b, width), F32)
        for k in range(0, reach, 2):
            columns = pl.ds(pl.multiple_of((firsts[u] + k) * b, b), 2 * b)
            inner = lax.dot_general(
                beside(q_one_ref[rows, :], q_two_ref[rows, :]),
                beside(x_ref[columns, :], one_ref[columns, :]),
                NT,
                preferred_element_type=F32,
            )
            inner_t = lax.dot_general(
                beside(x_ref[rows, :], one_ref[rows, :]),
                beside(q_one_ref[columns, :], q_two_ref[columns, :]),
                NT,
                preferred_element_type=F32,
            )
            squashed = score_ref[local, unit_rows(k, 2)]
            offset_t = jnp.concatenate(
                [offrow_ref[firsts[u] + k + i, 0:1, :] for i in range(2)], axis=1
            )
            chosen = jnp.where(
                squashed > 0.0, inner - twice(off_ref[rows, :]), inner_t - offset_t
            )
            pair = (6.0 * squashed * (1.0 - squashed * squashed) * chosen).astype(BF16)
            grad_m = grad_m + jnp.dot(
                pair, swapped_ref[columns, :], preferred_element_type=F32
            )
        mine = m_ref[local, :]
        dm_ref[local, :] = 3.0 * (1.0 - mine * mine) * grad_m
    grad = lax.dot_general(
        dm_ref[...],
        block_diagonal(proj_ref[...]),
        NT,
        precision=HIGHEST,
        preferred_element_type=F32,
    ).astype(BF16)
    for k in range(groups):
        sums_ref[k, :rows_v, :] = grad[k * rows_v : (k + 1) * rows_v]
    out_copy.wait()


def finish_kernel(got_ref, vector_ref, weight_ref):
    groups = got_ref.shape[0]
    rows_v = vector_ref.shape[0] // groups
    rows_w = weight_ref.shape[0] // groups
    for k in range(groups):
        got = got_ref[k].astype(F32)
        vector_ref[k * rows_v : (k + 1) * rows_v, :] = got[:rows_v]
        weight_ref[k * rows_w : (k + 1) * rows_w, :] = got[rows_v:]


def device_groups(counts, kept):
    strides = [math.prod(counts[i + 1 :]) for i in range(len(counts))]

    def spread(axes):
        numbers = [0]
        for i in axes:
            numbers = [n + k * strides[i] for n in numbers for k in range(counts[i])]
        return numbers

    others = [i for i in range(len(counts)) if i not in kept]
    return [[base + k for k in spread(kept)] for base in spread(others)]


def body(features, node_vectors, projections, mix_weight, region_sizes, cotangent):
    nodes, _, steps, width = features.shape
    axes = ("node", "win")
    node_count, win_count = lax.axis_size("node"), lax.axis_size("win")
    own_units = nodes // BLOCK
    units = own_units + 2 * HALO
    rim = HALO * BLOCK
    flat = nodes * steps
    row = steps * width
    in_vmem = pl.BlockSpec(memory_space=pltpu.VMEM)
    in_hbm = pl.BlockSpec(memory_space=pltpu.HBM)
    features, cotangent = features.reshape(flat, width), cotangent.reshape(flat, width)
    features, cotangent, node_vectors, projections, mix_weight = (
        pltpu.with_memory_space_constraint(array, pltpu.HBM)
        for array in (features, cotangent, node_vectors, projections, mix_weight)
    )
    own, far, near, learned, projections, mix_weight = pl.pallas_call(
        pack_kernel,
        name="pack",
        in_specs=[in_hbm] * 5,
        out_shape=(
            jax.ShapeDtypeStruct((nodes, 5 * width), BF16),
            jax.ShapeDtypeStruct((rim, 5 * width), BF16),
            jax.ShapeDtypeStruct((rim, 5 * width), BF16),
            jax.ShapeDtypeStruct((nodes, width), F32),
            jax.ShapeDtypeStruct(projections.shape, F32),
            jax.ShapeDtypeStruct(mix_weight.shape, BF16),
        ),
        scratch_shapes=[
            pltpu.VMEM((flat, width), BF16),
            pltpu.VMEM((flat, width), BF16),
            pltpu.VMEM((nodes, width), F32),
            pltpu.VMEM((flat, width), F32),
            pltpu.SemaphoreType.DMA((5,)),
        ],
        compiler_params=pltpu.CompilerParams(vmem_limit_bytes=16 << 20),
    )(features, cotangent, node_vectors, projections, mix_weight)
    border = [(i, i + 1) for i in range(1, node_count - 1, 2)]
    inside = [(i, i + 1) for i in range(0, node_count, 2)]
    near = lax.ppermute(near, "node", inside + [(j, i) for i, j in inside])
    far = lax.ppermute(far, "node", border + [(j, i) for i, j in border])
    lead = lax.axis_index("node") * own_units - HALO
    place = jnp.arange(units, dtype=jnp.int32)
    unit = lead + place
    ends = jnp.cumsum(region_sizes)
    passed = (ends[None, :] <= unit[:, None]).astype(jnp.int32)
    in_range = (unit >= 0) & (unit < node_count * own_units)
    region = jnp.where(in_range, jnp.sum(passed, axis=1), -1)
    first = jnp.sum(passed * region_sizes[None, :], axis=1) - lead
    first = jnp.clip(first, jnp.maximum(place - HALO, 0), jnp.minimum(place, units - HALO - 1))

    span = units * BLOCK
    y_far, y_near = 2, 2
    inner_count = node_count // (y_far * y_near)
    groups = y_far * win_count
    rows_v = nodes // groups
    rows_w = 3 * width // groups
    reach = (HALO + 1) * BLOCK
    in_smem = pl.BlockSpec(memory_space=pltpu.SMEM)
    out, sums = pl.pallas_call(
        partial(layer_kernel, 1.0 / math.sqrt(flat * node_count * win_count)),
        name="layer",
        in_specs=[in_smem] * 2 + [in_vmem] * 6,
        out_specs=(in_hbm, in_vmem),
        out_shape=(
            jax.ShapeDtypeStruct((flat, width), BF16),
            jax.ShapeDtypeStruct((groups, rows_v + rows_w, width), BF16),
        ),
        scratch_shapes=[
            pltpu.VMEM((span, row), BF16),
            pltpu.VMEM((span, row), BF16),
            pltpu.VMEM((span, width), BF16),
            pltpu.VMEM((span, width), BF16),
            pltpu.VMEM((span, reach), BF16),
            pltpu.VMEM((span, reach), BF16),
            pltpu.VMEM((nodes, reach), F32),
            pltpu.VMEM((span, width), F32),
            pltpu.VMEM((span, row), BF16),
            pltpu.VMEM((nodes, row), BF16),
            pltpu.VMEM((span, row), BF16),
            pltpu.VMEM((span, row), BF16),
            pltpu.VMEM((span, row), F32),
            pltpu.VMEM((span, width), F32),
            pltpu.VMEM((units, 8, width), F32),
            pltpu.VMEM((nodes, width), F32),
            pltpu.VMEM((flat, width), F32),
            pltpu.VMEM((flat, width), BF16),
            pltpu.SemaphoreType.DMA,
        ],
        compiler_params=pltpu.CompilerParams(vmem_limit_bytes=32 << 20),
        cost_estimate=pl.CostEstimate(
            flops=12 * span * reach * row, bytes_accessed=8 << 20, transcendentals=span * reach
        ),
    )(region, first, far, near, own, learned, projections, mix_weight)

    counts = (y_far, y_near, inner_count, win_count)
    outer_groups = device_groups(counts, (0, 3))
    inner_groups = device_groups(counts, (1, 2))
    exchange = partial(
        lax.all_to_all, axis_name=axes, split_axis=0, concat_axis=0, tiled=True
    )
    got = exchange(sums, axis_index_groups=outer_groups).astype(F32)
    vector_sum = jnp.sum(
        got[:, :rows_v].reshape(y_far, win_count, rows_v, width), axis=1
    ).astype(BF16)
    weight_sum = jnp.sum(got[:, rows_v:], axis=0).astype(BF16)
    shares = jnp.broadcast_to(weight_sum[None], (y_near * inner_count, rows_w, width))
    vector_sum, shares = lax.optimization_barrier((vector_sum, shares))
    got = exchange(shares, axis_index_groups=inner_groups).astype(F32)
    weight_sum = jnp.sum(got, axis=0).astype(BF16)
    back = jnp.concatenate(
        [
            jnp.broadcast_to(
                vector_sum[:, None], (y_far, win_count, rows_v, width)
            ).reshape(groups, rows_v, width),
            jnp.broadcast_to(weight_sum[None], (groups, rows_w, width)),
        ],
        axis=1,
    )
    got = exchange(back, axis_index_groups=outer_groups)
    vector_grad, weight_grad = pl.pallas_call(
        finish_kernel,
        name="finish",
        in_specs=[in_vmem],
        out_shape=(
            jax.ShapeDtypeStruct((nodes, width), F32),
            jax.ShapeDtypeStruct((3 * width, width), F32),
        ),
        compiler_params=pltpu.CompilerParams(vmem_limit_bytes=8 << 20),
    )(got)
    weight_grad = weight_grad.reshape(3, width, width)
    return (out.reshape(nodes, 1, steps, width), vector_grad, weight_grad)


def solution(mesh):
    placed = (
        P("node", "win", None, None),
        P("node", None),
        P(),
        P(),
        P(),
        P("node", "win", None, None),
    )
    return jax.shard_map(
        body,
        mesh=mesh,
        in_specs=placed,
        out_specs=(P("node", "win", None, None), P("node", None), P()),
        check_vma=False,
    )
```

```python
from functools import partial
import math

import jax
import jax.numpy as jnp
from jax import lax
from jax.experimental import pallas as pl
from jax.experimental.pallas import tpu as pltpu
from jax.sharding import PartitionSpec as P


BLOCK = 128
HALO = 3
KEEP_INPUT = 0.05
F32 = jnp.float32
BF16 = jnp.bfloat16
NT = (((1,), (1,)), ((), ()))
TN = (((0,), (0,)), ((), ()))
HIGHEST = lax.Precision.HIGHEST


def block_diagonal(projections):
    zero = jnp.zeros_like(projections[0])
    return jnp.concatenate(
        [
            jnp.concatenate([projections[0], zero], axis=1),
            jnp.concatenate([zero, projections[1]], axis=1),
        ],
        axis=0,
    )


def pack_kernel(
    x_hbm, g_hbm, nv_hbm, proj_hbm, mix_hbm, own_ref, far_ref, near_ref, m_ref, proj_ref, mix_ref,
    x_in, g_in, nv_in, flat_ref, sems,
):
    copies = [
        pltpu.make_async_copy(source, target, sems.at[i])
        for i, (source, target) in enumerate(
            (
                (x_hbm, x_in),
                (g_hbm, g_in),
                (nv_hbm, nv_in),
                (proj_hbm, proj_ref),
                (mix_hbm, mix_ref),
            )
        )
    ]
    for copy in copies:
        copy.start()
    nodes, width = m_ref.shape
    rim = far_ref.shape[0]
    for part, source in enumerate((x_in, g_in)):
        copies[part].wait()
        flat_ref[...] = source[...].astype(F32)
        for step in range(2):
            rows = flat_ref[pl.ds(step, nodes, stride=2), :].astype(BF16)
            first = (1 + 2 * part + step) * width
            own_ref[:, first : first + width] = rows
    copies[2].wait()
    copies[3].wait()
    learned = jnp.tanh(
        3.0
        * jnp.dot(
            nv_in[...],
            block_diagonal(proj_ref[...]),
            precision=HIGHEST,
            preferred_element_type=F32,
        )
    )
    m_ref[...] = learned
    own_ref[:, :width] = learned.astype(BF16)
    odd = lax.rem(lax.axis_index("node"), 2)
    gap = nodes - rim
    far_ref[...] = own_ref[pl.ds(pl.multiple_of(odd * gap, BLOCK), rim), :]
    near_ref[...] = own_ref[pl.ds(pl.multiple_of((1 - odd) * gap, BLOCK), rim), :]
    copies[4].wait()


def unit_rows(first, count=1):
    return slice(first * BLOCK, (first + count) * BLOCK)


def rim_places(rim, nodes):
    odd = lax.rem(lax.axis_index("node"), 2)
    span = rim + nodes
    return (
        pl.ds(pl.multiple_of(odd * span, BLOCK), rim),
        pl.ds(pl.multiple_of((1 - odd) * span, BLOCK), rim),
    )


def beside(left, right):
    return jnp.concatenate([left, right], axis=1)


def twice(values):
    return beside(values, values)


def turned(learned):
    width = learned.shape[1]
    half = width // 2
    i = lax.broadcasted_iota(jnp.int32, (width, width), 0)
    j = lax.broadcasted_iota(jnp.int32, (width, width), 1)
    turn = jnp.where(i == j + half, 1.0, 0.0) - jnp.where(j == i + half, 1.0, 0.0)
    return jnp.dot(learned, turn.astype(BF16), preferred_element_type=F32).astype(BF16)


def layer_kernel(
    norm_scale,
    region_ref,
    first_ref,
    far_ref,
    near_ref,
    own_ref,
    m_ref,
    proj_ref,
    mix_ref,
    out_hbm,
    sums_ref,
    x_ref,
    g_ref,
    learned_ref,
    swapped_ref,
    adj_ref,
    adjt_ref,
    score_ref,
    rdeg_ref,
    one_ref,
    two_ref,
    q_one_ref,
    q_two_ref,
    back_ref,
    off_ref,
    offrow_ref,
    dm_ref,
    flat_ref,
    out_ref,
    sem,
):
    b = BLOCK
    nodes = own_ref.shape[0]
    rim, width = far_ref.shape[0], m_ref.shape[1]
    own_units = nodes // b
    units = own_units + 2 * HALO
    reach = HALO + 1
    row = 2 * width
    keep = 1.0 - KEEP_INPUT
    far_place, near_place = rim_places(rim, nodes)
    own_place = pl.ds(rim, nodes)
    for place, source in ((far_place, far_ref), (own_place, own_ref), (near_place, near_ref)):
        learned = source[:, :width]
        learned_ref[place, :] = learned
        swapped_ref[place, :] = turned(learned)
        x_ref[place, :] = source[:, width : width + row]
        g_ref[place, :] = source[:, width + row :]

    firsts = [first_ref[u] for u in range(units)]
    windows = [pl.ds(pl.multiple_of(firsts[u] * b, b), reach * b) for u in range(units)]
    own_first = HALO
    own_last = own_first + own_units
    mixed = jnp.concatenate([mix_ref[2], mix_ref[1]], axis=0)
    for u in range(units):
        rows = unit_rows(u)
        mine = region_ref[u]
        total = jnp.zeros((b, b), F32)
        for k in range(reach):
            other = firsts[u] + k
            scores = lax.dot_general(
                learned_ref[rows, :],
                swapped_ref[pl.ds(pl.multiple_of(other * b, b), b), :],
                NT,
                preferred_element_type=F32,
            )
            same = jnp.where((region_ref[other] == mine) & (mine >= 0), 3.0, 0.0)
            squashed = jnp.tanh(scores * same)
            positive = jnp.maximum(squashed, 0.0)
            negative = jnp.minimum(squashed, 0.0)
            forward = positive * positive
            columns = unit_rows(k)
            if own_first <= u < own_last:
                score_ref[unit_rows(u - own_first), columns] = squashed
            adj_ref[rows, columns] = forward.astype(BF16)
            adjt_ref[rows, columns] = (negative * negative).astype(BF16)
            total = total + forward
        degree = 1.0 + jnp.sum(total, axis=1, keepdims=True)
        rdeg = jnp.broadcast_to(1.0 / degree, (b, width))
        rdeg_ref[rows, :] = rdeg
        for s in range(2):
            cut = slice(s * width, (s + 1) * width)
            back = lax.dot_general(g_ref[rows, cut], mixed, NT, preferred_element_type=F32)
            q_two_ref[rows, cut] = (keep * back[:, :width] * rdeg).astype(BF16)
            back_ref[rows, cut] = back[:, width:]
    order = list(range(own_first, own_last))
    order += [u for u in range(units) if u not in order]
    for u in order:
        rows = unit_rows(u)
        rdeg = twice(rdeg_ref[rows, :])
        carried = jnp.dot(
            adjt_ref[rows, :], q_two_ref[windows[u], :], preferred_element_type=F32
        )
        mine = x_ref[rows, :].astype(F32)
        prop = jnp.dot(adj_ref[rows, :], x_ref[windows[u], :], preferred_element_type=F32)
        prop = (prop + mine) * rdeg
        one_ref[rows, :] = (KEEP_INPUT * mine + keep * prop).astype(BF16)
        carried = carried + q_two_ref[rows, :].astype(F32)
        grad_one = (keep * (back_ref[rows, :] + carried) * rdeg).astype(BF16)
        q_one_ref[rows, :] = grad_one
        inner = grad_one.astype(F32) * prop
        off_ref[rows, :] = inner[:, :width] + inner[:, width:]

    def second_hop(u):
        rows = unit_rows(u)
        prop = jnp.dot(adj_ref[rows, :], one_ref[windows[u], :], preferred_element_type=F32)
        prop = (prop + one_ref[rows, :].astype(F32)) * twice(rdeg_ref[rows, :])
        inner = q_two_ref[rows, :].astype(F32) * prop
        inner = off_ref[rows, :] + inner[:, :width] + inner[:, width:]
        offset = jnp.broadcast_to(jnp.sum(inner, axis=1, keepdims=True), (b, width))
        off_ref[rows, :] = offset
        offrow_ref[u] = jnp.transpose(offset)[:8]
        if own_first <= u < own_last:
            two_ref[unit_rows(u - own_first), :] = (
                KEEP_INPUT * x_ref[rows, :].astype(F32) + keep * prop
            ).astype(BF16)

    for u in range(own_first, own_last):
        second_hop(u)
    weights = jnp.concatenate([mix_ref[0], mix_ref[1], mix_ref[2]], axis=0)
    all_hops, all_up = [], []
    for s in range(2):
        cut = slice(s * width, (s + 1) * width)
        all_hops.append(
            jnp.concatenate(
                [x_ref[own_place, cut], one_ref[own_place, cut], two_ref[:, cut]], axis=1
            )
        )
        all_up.append(g_ref[own_place, cut])
        flat_ref[pl.ds(s, nodes, stride=2), :] = jnp.dot(
            all_hops[s], weights, preferred_element_type=F32
        )
    out_ref[...] = flat_ref[...].astype(BF16)
    out_copy = pltpu.make_async_copy(out_ref, out_hbm, sem)
    out_copy.start()
    for u in range(units):
        if not own_first <= u < own_last:
            second_hop(u)
    groups = sums_ref.shape[0]
    rows_v = nodes // groups
    rows_w = 3 * width // groups
    weight = norm_scale * lax.dot_general(
        jnp.concatenate(all_hops, axis=0),
        jnp.concatenate(all_up, axis=0),
        TN,
        preferred_element_type=F32,
    )
    for k in range(groups):
        sums_ref[k, rows_v:, :] = weight[k * rows_w : (k + 1) * rows_w].astype(BF16)

    for u in range(own_first, own_last):
        rows = unit_rows(u)
        local = unit_rows(u - own_first)
        grad_m = jnp.zeros((b, width), F32)
        for k in range(0, reach, 2):
            columns = pl.ds(pl.multiple_of((firsts[u] + k) * b, b), 2 * b)
            inner = lax.dot_general(
                beside(q_one_ref[rows, :], q_two_ref[rows, :]),
                beside(x_ref[columns, :], one_ref[columns, :]),
                NT,
                preferred_element_type=F32,
            )
            inner_t = lax.dot_general(
                beside(x_ref[rows, :], one_ref[rows, :]),
                beside(q_one_ref[columns, :], q_two_ref[columns, :]),
                NT,
                preferred_element_type=F32,
            )
            squashed = score_ref[local, unit_rows(k, 2)]
            offset_t = jnp.concatenate(
                [offrow_ref[firsts[u] + k + i, 0:1, :] for i in range(2)], axis=1
            )
            chosen = jnp.where(
                squashed > 0.0, inner - twice(off_ref[rows, :]), inner_t - offset_t
            )
            pair = (6.0 * squashed * (1.0 - squashed * squashed) * chosen).astype(BF16)
            grad_m = grad_m + jnp.dot(
                pair, swapped_ref[columns, :], preferred_element_type=F32
            )
        mine = m_ref[local, :]
        dm_ref[local, :] = 3.0 * (1.0 - mine * mine) * grad_m
    grad = lax.dot_general(
        dm_ref[...],
        block_diagonal(proj_ref[...]),
        NT,
        precision=HIGHEST,
        preferred_element_type=F32,
    ).astype(BF16)
    for k in range(groups):
        sums_ref[k, :rows_v, :] = grad[k * rows_v : (k + 1) * rows_v]
    out_copy.wait()


def finish_kernel(got_ref, vector_ref, weight_ref):
    groups = got_ref.shape[0]
    rows_v = vector_ref.shape[0] // groups
    rows_w = weight_ref.shape[0] // groups
    for k in range(groups):
        got = got_ref[k].astype(F32)
        vector_ref[k * rows_v : (k + 1) * rows_v, :] = got[:rows_v]
        weight_ref[k * rows_w : (k + 1) * rows_w, :] = got[rows_v:]


def device_groups(counts, kept):
    strides = [math.prod(counts[i + 1 :]) for i in range(len(counts))]

    def spread(axes):
        numbers = [0]
        for i in axes:
            numbers = [n + k * strides[i] for n in numbers for k in range(counts[i])]
        return numbers

    others = [i for i in range(len(counts)) if i not in kept]
    return [[base + k for k in spread(kept)] for base in spread(others)]


def body(features, node_vectors, projections, mix_weight, region_sizes, cotangent):
    nodes, _, steps, width = features.shape
    axes = ("node", "win")
    node_count, win_count = lax.axis_size("node"), lax.axis_size("win")
    own_units = nodes // BLOCK
    units = own_units + 2 * HALO
    rim = HALO * BLOCK
    flat = nodes * steps
    row = steps * width
    in_vmem = pl.BlockSpec(memory_space=pltpu.VMEM)
    in_hbm = pl.BlockSpec(memory_space=pltpu.HBM)
    features, cotangent = features.reshape(flat, width), cotangent.reshape(flat, width)
    features, cotangent, node_vectors, projections, mix_weight = (
        pltpu.with_memory_space_constraint(array, pltpu.HBM)
        for array in (features, cotangent, node_vectors, projections, mix_weight)
    )
    own, far, near, learned, projections, mix_weight = pl.pallas_call(
        pack_kernel,
        name="pack",
        in_specs=[in_hbm] * 5,
        out_shape=(
            jax.ShapeDtypeStruct((nodes, 5 * width), BF16),
            jax.ShapeDtypeStruct((rim, 5 * width), BF16),
            jax.ShapeDtypeStruct((rim, 5 * width), BF16),
            jax.ShapeDtypeStruct((nodes, width), F32),
            jax.ShapeDtypeStruct(projections.shape, F32),
            jax.ShapeDtypeStruct(mix_weight.shape, BF16),
        ),
        scratch_shapes=[
            pltpu.VMEM((flat, width), BF16),
            pltpu.VMEM((flat, width), BF16),
            pltpu.VMEM((nodes, width), F32),
            pltpu.VMEM((flat, width), F32),
            pltpu.SemaphoreType.DMA((5,)),
        ],
        compiler_params=pltpu.CompilerParams(vmem_limit_bytes=16 << 20),
    )(features, cotangent, node_vectors, projections, mix_weight)
    border = [(i, i + 1) for i in range(1, node_count - 1, 2)]
    inside = [(i, i + 1) for i in range(0, node_count, 2)]
    far = lax.ppermute(far, "node", border + [(j, i) for i, j in border])
    near = lax.ppermute(near, "node", inside + [(j, i) for i, j in inside])
    lead = lax.axis_index("node") * own_units - HALO
    place = jnp.arange(units, dtype=jnp.int32)
    unit = lead + place
    ends = jnp.cumsum(region_sizes)
    passed = (ends[None, :] <= unit[:, None]).astype(jnp.int32)
    in_range = (unit >= 0) & (unit < node_count * own_units)
    region = jnp.where(in_range, jnp.sum(passed, axis=1), -1)
    first = jnp.sum(passed * region_sizes[None, :], axis=1) - lead
    first = jnp.clip(
        first, jnp.maximum(place - HALO, 0), jnp.minimum(place, units - HALO - 1)
    )

    span = units * BLOCK
    y_far, y_near = 2, 2
    inner_count = node_count // (y_far * y_near)
    groups = y_far * win_count
    rows_v = nodes // groups
    rows_w = 3 * width // groups
    reach = (HALO + 1) * BLOCK
    in_smem = pl.BlockSpec(memory_space=pltpu.SMEM)
    out, sums = pl.pallas_call(
        partial(layer_kernel, 1.0 / math.sqrt(flat * node_count * win_count)),
        name="layer",
        in_specs=[in_smem] * 2 + [in_vmem] * 6,
        out_specs=(in_hbm, in_vmem),
        out_shape=(
            jax.ShapeDtypeStruct((flat, width), BF16),
            jax.ShapeDtypeStruct((groups, rows_v + rows_w, width), BF16),
        ),
        scratch_shapes=[
            pltpu.VMEM((span, row), BF16),
            pltpu.VMEM((span, row), BF16),
            pltpu.VMEM((span, width), BF16),
            pltpu.VMEM((span, width), BF16),
            pltpu.VMEM((span, reach), BF16),
            pltpu.VMEM((span, reach), BF16),
            pltpu.VMEM((nodes, reach), F32),
            pltpu.VMEM((span, width), F32),
            pltpu.VMEM((span, row), BF16),
            pltpu.VMEM((nodes, row), BF16),
            pltpu.VMEM((span, row), BF16),
            pltpu.VMEM((span, row), BF16),
            pltpu.VMEM((span, row), F32),
            pltpu.VMEM((span, width), F32),
            pltpu.VMEM((units, 8, width), F32),
            pltpu.VMEM((nodes, width), F32),
            pltpu.VMEM((flat, width), F32),
            pltpu.VMEM((flat, width), BF16),
            pltpu.SemaphoreType.DMA,
        ],
        compiler_params=pltpu.CompilerParams(vmem_limit_bytes=32 << 20),
        cost_estimate=pl.CostEstimate(
            flops=12 * span * reach * row, bytes_accessed=8 << 20, transcendentals=span * reach
        ),
    )(region, first, far, near, own, learned, projections, mix_weight)

    counts = (y_far, y_near, inner_count, win_count)
    outer_groups = device_groups(counts, (0, 3))
    inner_groups = device_groups(counts, (1, 2))
    exchange = partial(
        lax.all_to_all, axis_name=axes, split_axis=0, concat_axis=0, tiled=True
    )
    got = exchange(sums, axis_index_groups=outer_groups).astype(F32)
    vector_sum = jnp.sum(
        got[:, :rows_v].reshape(y_far, win_count, rows_v, width), axis=1
    ).astype(BF16)
    weight_sum = jnp.sum(got[:, rows_v:], axis=0).astype(BF16)
    shares = jnp.broadcast_to(weight_sum[None], (y_near * inner_count, rows_w, width))
    vector_sum, shares = lax.optimization_barrier((vector_sum, shares))
    got = exchange(shares, axis_index_groups=inner_groups).astype(F32)
    weight_sum = jnp.sum(got, axis=0).astype(BF16)
    back = jnp.concatenate(
        [
            jnp.broadcast_to(
                vector_sum[:, None], (y_far, win_count, rows_v, width)
            ).reshape(groups, rows_v, width),
            jnp.broadcast_to(weight_sum[None], (groups, rows_w, width)),
        ],
        axis=1,
    )
    got = exchange(back, axis_index_groups=outer_groups)
    vector_grad, weight_grad = pl.pallas_call(
        finish_kernel,
        name="finish",
        in_specs=[in_vmem],
        out_shape=(
            jax.ShapeDtypeStruct((nodes, width), F32),
            jax.ShapeDtypeStruct((3 * width, width), F32),
        ),
        compiler_params=pltpu.CompilerParams(vmem_limit_bytes=8 << 20),
    )(got)
    weight_grad = weight_grad.reshape(3, width, width)
    return (out.reshape(nodes, 1, steps, width), vector_grad, weight_grad)


def solution(mesh):
    placed = (
        P("node", "win", None, None),
        P("node", None),
        P(),
        P(),
        P(),
        P("node", "win", None, None),
    )
    return jax.shard_map(
        body,
        mesh=mesh,
        in_specs=placed,
        out_specs=(P("node", "win", None, None), P("node", None), P()),
        check_vma=False,
    )
```

```python
from functools import partial
import math

import jax
import jax.numpy as jnp
from jax import lax
from jax.experimental import pallas as pl
from jax.experimental.pallas import tpu as pltpu
from jax.sharding import PartitionSpec as P


BLOCK = 128
HALO = 3
KEEP_INPUT = 0.05
F32 = jnp.float32
BF16 = jnp.bfloat16
NT = (((1,), (1,)), ((), ()))
TN = (((0,), (0,)), ((), ()))


def block_diagonal(projections):
    zero = jnp.zeros_like(projections[0])
    return jnp.concatenate(
        [
            jnp.concatenate([projections[0], zero], axis=1),
            jnp.concatenate([zero, projections[1]], axis=1),
        ],
        axis=0,
    )


def split_product(left, right, dims):
    (left_axis,), (right_axis,) = dims[0]
    high, other = left.astype(BF16), right.astype(BF16)
    low = (left - high.astype(F32)).astype(BF16)
    rest = (right - other.astype(F32)).astype(BF16)
    return lax.dot_general(
        jnp.concatenate([high, high, low], axis=left_axis),
        jnp.concatenate([other, rest, other], axis=right_axis),
        dims,
        preferred_element_type=F32,
    )


def pack_kernel(
    x_hbm, g_hbm, nv_hbm, proj_hbm, mix_hbm, own_ref, far_ref, near_ref, m_ref, proj_ref, mix_ref,
    x_in, g_in, nv_in, flat_ref, sems,
):
    copies = [
        pltpu.make_async_copy(source, target, sems.at[i])
        for i, (source, target) in enumerate(
            (
                (x_hbm, x_in),
                (g_hbm, g_in),
                (nv_hbm, nv_in),
                (proj_hbm, proj_ref),
                (mix_hbm, mix_ref),
            )
        )
    ]
    for copy in copies:
        copy.start()
    nodes, width = m_ref.shape
    rim = far_ref.shape[0]
    for part, source in enumerate((x_in, g_in)):
        copies[part].wait()
        flat_ref[...] = source[...].astype(F32)
        for step in range(2):
            rows = flat_ref[pl.ds(step, nodes, stride=2), :].astype(BF16)
            first = (1 + 2 * part + step) * width
            own_ref[:, first : first + width] = rows
    copies[2].wait()
    copies[3].wait()
    learned = jnp.tanh(
        3.0 * split_product(nv_in[...], block_diagonal(proj_ref[...]), (((1,), (0,)), ((), ())))
    )
    m_ref[...] = learned
    own_ref[:, :width] = learned.astype(BF16)
    odd = lax.rem(lax.axis_index("node"), 2)
    gap = nodes - rim
    far_ref[...] = own_ref[pl.ds(pl.multiple_of(odd * gap, BLOCK), rim), :]
    near_ref[...] = own_ref[pl.ds(pl.multiple_of((1 - odd) * gap, BLOCK), rim), :]
    copies[4].wait()


def unit_rows(first, count=1):
    return slice(first * BLOCK, (first + count) * BLOCK)


def rim_places(rim, nodes):
    odd = lax.rem(lax.axis_index("node"), 2)
    span = rim + nodes
    return (
        pl.ds(pl.multiple_of(odd * span, BLOCK), rim),
        pl.ds(pl.multiple_of((1 - odd) * span, BLOCK), rim),
    )


def beside(left, right):
    return jnp.concatenate([left, right], axis=1)


def twice(values):
    return beside(values, values)


def turned(learned):
    width = learned.shape[1]
    half = width // 2
    i = lax.broadcasted_iota(jnp.int32, (width, width), 0)
    j = lax.broadcasted_iota(jnp.int32, (width, width), 1)
    turn = jnp.where(i == j + half, 1.0, 0.0) - jnp.where(j == i + half, 1.0, 0.0)
    return jnp.dot(learned, turn.astype(BF16), preferred_element_type=F32).astype(BF16)


def layer_kernel(
    norm_scale,
    region_ref,
    first_ref,
    far_ref,
    near_ref,
    own_ref,
    m_ref,
    proj_ref,
    mix_ref,
    out_hbm,
    sums_ref,
    x_ref,
    g_ref,
    learned_ref,
    swapped_ref,
    adj_ref,
    adjt_ref,
    score_ref,
    rdeg_ref,
    one_ref,
    two_ref,
    q_one_ref,
    q_two_ref,
    back_ref,
    off_ref,
    offrow_ref,
    dm_ref,
    flat_ref,
    out_ref,
    sem,
):
    b = BLOCK
    nodes = own_ref.shape[0]
    rim, width = far_ref.shape[0], m_ref.shape[1]
    own_units = nodes // b
    units = own_units + 2 * HALO
    reach = HALO + 1
    row = 2 * width
    keep = 1.0 - KEEP_INPUT
    far_place, near_place = rim_places(rim, nodes)
    own_place = pl.ds(rim, nodes)
    for place, source in ((far_place, far_ref), (own_place, own_ref), (near_place, near_ref)):
        learned = source[:, :width]
        learned_ref[place, :] = learned
        swapped_ref[place, :] = turned(learned)
        x_ref[place, :] = source[:, width : width + row]
        g_ref[place, :] = source[:, width + row :]

    firsts = [first_ref[u] for u in range(units)]
    windows = [pl.ds(pl.multiple_of(firsts[u] * b, b), reach * b) for u in range(units)]
    own_first = HALO
    own_last = own_first + own_units
    mixed = jnp.concatenate([mix_ref[2], mix_ref[1]], axis=0)
    for u in range(units):
        rows = unit_rows(u)
        mine = region_ref[u]
        total = jnp.zeros((b, b), F32)
        for k in range(0, reach, 2):
            other = firsts[u] + k
            pair_scores = lax.dot_general(
                learned_ref[rows, :],
                swapped_ref[pl.ds(pl.multiple_of(other * b, b), 2 * b), :],
                NT,
                preferred_element_type=F32,
            )
            for i in range(2):
                same = jnp.where((region_ref[other + i] == mine) & (mine >= 0), 3.0, 0.0)
                squashed = jnp.tanh(pair_scores[:, i * b : (i + 1) * b] * same)
                positive = jnp.maximum(squashed, 0.0)
                negative = jnp.minimum(squashed, 0.0)
                forward = positive * positive
                columns = unit_rows(k + i)
                if own_first <= u < own_last:
                    score_ref[unit_rows(u - own_first), columns] = squashed
                adj_ref[rows, columns] = forward.astype(BF16)
                adjt_ref[rows, columns] = (negative * negative).astype(BF16)
                total = total + forward
        degree = 1.0 + jnp.sum(total, axis=1, keepdims=True)
        rdeg = jnp.broadcast_to(1.0 / degree, (b, width))
        rdeg_ref[rows, :] = rdeg
        for s in range(2):
            cut = slice(s * width, (s + 1) * width)
            back = lax.dot_general(g_ref[rows, cut], mixed, NT, preferred_element_type=F32)
            q_two_ref[rows, cut] = (keep * back[:, :width] * rdeg).astype(BF16)
            back_ref[rows, cut] = back[:, width:]
    order = list(range(own_first, own_last))
    order += [u for u in range(units) if u not in order]
    for u in order:
        rows = unit_rows(u)
        rdeg = twice(rdeg_ref[rows, :])
        carried = jnp.dot(
            adjt_ref[rows, :], q_two_ref[windows[u], :], preferred_element_type=F32
        )
        mine = x_ref[rows, :].astype(F32)
        prop = jnp.dot(adj_ref[rows, :], x_ref[windows[u], :], preferred_element_type=F32)
        prop = (prop + mine) * rdeg
        one_ref[rows, :] = (KEEP_INPUT * mine + keep * prop).astype(BF16)
        carried = carried + q_two_ref[rows, :].astype(F32)
        grad_one = (keep * (back_ref[rows, :] + carried) * rdeg).astype(BF16)
        q_one_ref[rows, :] = grad_one
        inner = grad_one.astype(F32) * prop
        off_ref[rows, :] = inner[:, :width] + inner[:, width:]

    def second_hop(u):
        rows = unit_rows(u)
        prop = jnp.dot(adj_ref[rows, :], one_ref[windows[u], :], preferred_element_type=F32)
        prop = (prop + one_ref[rows, :].astype(F32)) * twice(rdeg_ref[rows, :])
        inner = q_two_ref[rows, :].astype(F32) * prop
        inner = off_ref[rows, :] + inner[:, :width] + inner[:, width:]
        offset = jnp.broadcast_to(jnp.sum(inner, axis=1, keepdims=True), (b, width))
        off_ref[rows, :] = offset
        offrow_ref[u] = jnp.transpose(offset)[:8]
        if own_first <= u < own_last:
            two_ref[unit_rows(u - own_first), :] = (
                KEEP_INPUT * x_ref[rows, :].astype(F32) + keep * prop
            ).astype(BF16)

    for u in range(own_first, own_last):
        second_hop(u)
    weights = jnp.concatenate([mix_ref[0], mix_ref[1], mix_ref[2]], axis=0)
    all_hops, all_up = [], []
    for s in range(2):
        cut = slice(s * width, (s + 1) * width)
        all_hops.append(
            jnp.concatenate(
                [x_ref[own_place, cut], one_ref[own_place, cut], two_ref[:, cut]], axis=1
            )
        )
        all_up.append(g_ref[own_place, cut])
        flat_ref[pl.ds(s, nodes, stride=2), :] = jnp.dot(
            all_hops[s], weights, preferred_element_type=F32
        )
    out_ref[...] = flat_ref[...].astype(BF16)
    out_copy = pltpu.make_async_copy(out_ref, out_hbm, sem)
    out_copy.start()
    for u in range(units):
        if not own_first <= u < own_last:
            second_hop(u)
    groups = sums_ref.shape[0]
    rows_v = nodes // groups
    rows_w = 3 * width // groups
    weight = norm_scale * lax.dot_general(
        jnp.concatenate(all_hops, axis=0),
        jnp.concatenate(all_up, axis=0),
        TN,
        preferred_element_type=F32,
    )
    for k in range(groups):
        sums_ref[k, rows_v:, :] = weight[k * rows_w : (k + 1) * rows_w].astype(BF16)

    for u in range(own_first, own_last):
        rows = unit_rows(u)
        local = unit_rows(u - own_first)
        grad_m = jnp.zeros((b, width), F32)
        for k in range(0, reach, 2):
            columns = pl.ds(pl.multiple_of((firsts[u] + k) * b, b), 2 * b)
            inner = lax.dot_general(
                beside(q_one_ref[rows, :], q_two_ref[rows, :]),
                beside(x_ref[columns, :], one_ref[columns, :]),
                NT,
                preferred_element_type=F32,
            )
            inner_t = lax.dot_general(
                beside(x_ref[rows, :], one_ref[rows, :]),
                beside(q_one_ref[columns, :], q_two_ref[columns, :]),
                NT,
                preferred_element_type=F32,
            )
            squashed = score_ref[local, unit_rows(k, 2)]
            offset_t = jnp.concatenate(
                [offrow_ref[firsts[u] + k + i, 0:1, :] for i in range(2)], axis=1
            )
            chosen = jnp.where(
                squashed > 0.0, inner - twice(off_ref[rows, :]), inner_t - offset_t
            )
            pair = (6.0 * squashed * (1.0 - squashed * squashed) * chosen).astype(BF16)
            grad_m = grad_m + jnp.dot(
                pair, swapped_ref[columns, :], preferred_element_type=F32
            )
        mine = m_ref[local, :]
        dm_ref[local, :] = 3.0 * (1.0 - mine * mine) * grad_m
    grad = split_product(dm_ref[...], block_diagonal(proj_ref[...]), NT).astype(BF16)
    for k in range(groups):
        sums_ref[k, :rows_v, :] = grad[k * rows_v : (k + 1) * rows_v]
    out_copy.wait()


def finish_kernel(got_ref, vector_ref, weight_ref):
    groups = got_ref.shape[0]
    rows_v = vector_ref.shape[0] // groups
    rows_w = weight_ref.shape[0] // groups
    for k in range(groups):
        got = got_ref[k].astype(F32)
        vector_ref[k * rows_v : (k + 1) * rows_v, :] = got[:rows_v]
        weight_ref[k * rows_w : (k + 1) * rows_w, :] = got[rows_v:]


def device_groups(counts, kept):
    strides = [math.prod(counts[i + 1 :]) for i in range(len(counts))]

    def spread(axes):
        numbers = [0]
        for i in axes:
            numbers = [n + k * strides[i] for n in numbers for k in range(counts[i])]
        return numbers

    others = [i for i in range(len(counts)) if i not in kept]
    return [[base + k for k in spread(kept)] for base in spread(others)]


def body(features, node_vectors, projections, mix_weight, region_sizes, cotangent):
    nodes, _, steps, width = features.shape
    axes = ("node", "win")
    node_count, win_count = lax.axis_size("node"), lax.axis_size("win")
    own_units = nodes // BLOCK
    units = own_units + 2 * HALO
    rim = HALO * BLOCK
    flat = nodes * steps
    row = steps * width
    in_vmem = pl.BlockSpec(memory_space=pltpu.VMEM)
    in_hbm = pl.BlockSpec(memory_space=pltpu.HBM)
    features, cotangent = features.reshape(flat, width), cotangent.reshape(flat, width)
    features, cotangent, node_vectors, projections, mix_weight = (
        pltpu.with_memory_space_constraint(array, pltpu.HBM)
        for array in (features, cotangent, node_vectors, projections, mix_weight)
    )
    own, far, near, learned, projections, mix_weight = pl.pallas_call(
        pack_kernel,
        name="pack",
        in_specs=[in_hbm] * 5,
        out_shape=(
            jax.ShapeDtypeStruct((nodes, 5 * width), BF16),
            jax.ShapeDtypeStruct((rim, 5 * width), BF16),
            jax.ShapeDtypeStruct((rim, 5 * width), BF16),
            jax.ShapeDtypeStruct((nodes, width), F32),
            jax.ShapeDtypeStruct(projections.shape, F32),
            jax.ShapeDtypeStruct(mix_weight.shape, BF16),
        ),
        scratch_shapes=[
            pltpu.VMEM((flat, width), BF16),
            pltpu.VMEM((flat, width), BF16),
            pltpu.VMEM((nodes, width), F32),
            pltpu.VMEM((flat, width), F32),
            pltpu.SemaphoreType.DMA((5,)),
        ],
        compiler_params=pltpu.CompilerParams(vmem_limit_bytes=16 << 20),
    )(features, cotangent, node_vectors, projections, mix_weight)
    border = [(i, i + 1) for i in range(1, node_count - 1, 2)]
    inside = [(i, i + 1) for i in range(0, node_count, 2)]
    far = lax.ppermute(far, "node", border + [(j, i) for i, j in border])
    near = lax.ppermute(near, "node", inside + [(j, i) for i, j in inside])
    lead = lax.axis_index("node") * own_units - HALO
    place = jnp.arange(units, dtype=jnp.int32)
    unit = lead + place
    ends = jnp.cumsum(region_sizes)
    passed = (ends[None, :] <= unit[:, None]).astype(jnp.int32)
    in_range = (unit >= 0) & (unit < node_count * own_units)
    region = jnp.where(in_range, jnp.sum(passed, axis=1), -1)
    first = jnp.sum(passed * region_sizes[None, :], axis=1) - lead
    first = jnp.clip(first, jnp.maximum(place - HALO, 0), jnp.minimum(place, units - HALO - 1))

    span = units * BLOCK
    y_far, y_near = 4, 1
    inner_count = node_count // (y_far * y_near)
    groups = y_far * win_count
    rows_v = nodes // groups
    rows_w = 3 * width // groups
    reach = (HALO + 1) * BLOCK
    in_smem = pl.BlockSpec(memory_space=pltpu.SMEM)
    out, sums = pl.pallas_call(
        partial(layer_kernel, 1.0 / math.sqrt(flat * node_count * win_count)),
        name="layer",
        in_specs=[in_smem] * 2 + [in_vmem] * 6,
        out_specs=(in_hbm, in_vmem),
        out_shape=(
            jax.ShapeDtypeStruct((flat, width), BF16),
            jax.ShapeDtypeStruct((groups, rows_v + rows_w, width), BF16),
        ),
        scratch_shapes=[
            pltpu.VMEM((span, row), BF16),
            pltpu.VMEM((span, row), BF16),
            pltpu.VMEM((span, width), BF16),
            pltpu.VMEM((span, width), BF16),
            pltpu.VMEM((span, reach), BF16),
            pltpu.VMEM((span, reach), BF16),
            pltpu.VMEM((nodes, reach), F32),
            pltpu.VMEM((span, width), F32),
            pltpu.VMEM((span, row), BF16),
            pltpu.VMEM((nodes, row), BF16),
            pltpu.VMEM((span, row), BF16),
            pltpu.VMEM((span, row), BF16),
            pltpu.VMEM((span, row), F32),
            pltpu.VMEM((span, width), F32),
            pltpu.VMEM((units, 8, width), F32),
            pltpu.VMEM((nodes, width), F32),
            pltpu.VMEM((flat, width), F32),
            pltpu.VMEM((flat, width), BF16),
            pltpu.SemaphoreType.DMA,
        ],
        compiler_params=pltpu.CompilerParams(vmem_limit_bytes=32 << 20),
        cost_estimate=pl.CostEstimate(
            flops=12 * span * reach * row, bytes_accessed=8 << 20, transcendentals=span * reach
        ),
    )(region, first, far, near, own, learned, projections, mix_weight)

    counts = (y_far, y_near, inner_count, win_count)
    outer_groups = device_groups(counts, (0, 3))
    inner_groups = device_groups(counts, (1, 2))
    exchange = partial(
        lax.all_to_all, axis_name=axes, split_axis=0, concat_axis=0, tiled=True
    )
    got = exchange(sums, axis_index_groups=outer_groups).astype(F32)
    vector_sum = jnp.sum(
        got[:, :rows_v].reshape(y_far, win_count, rows_v, width), axis=1
    ).astype(BF16)
    weight_sum = jnp.sum(got[:, rows_v:], axis=0).astype(BF16)
    shares = jnp.broadcast_to(weight_sum[None], (y_near * inner_count, rows_w, width))
    vector_sum, shares = lax.optimization_barrier((vector_sum, shares))
    got = exchange(shares, axis_index_groups=inner_groups).astype(F32)
    weight_sum = jnp.sum(got, axis=0).astype(BF16)
    back = jnp.concatenate(
        [
            jnp.broadcast_to(
                vector_sum[:, None], (y_far, win_count, rows_v, width)
            ).reshape(groups, rows_v, width),
            jnp.broadcast_to(weight_sum[None], (groups, rows_w, width)),
        ],
        axis=1,
    )
    got = exchange(back, axis_index_groups=outer_groups)
    vector_grad, weight_grad = pl.pallas_call(
        finish_kernel,
        name="finish",
        in_specs=[in_vmem],
        out_shape=(
            jax.ShapeDtypeStruct((nodes, width), F32),
            jax.ShapeDtypeStruct((3 * width, width), F32),
        ),
        compiler_params=pltpu.CompilerParams(vmem_limit_bytes=8 << 20),
    )(got)
    weight_grad = weight_grad.reshape(3, width, width)
    return (out.reshape(nodes, 1, steps, width), vector_grad, weight_grad)


def solution(mesh):
    placed = (
        P("node", "win", None, None),
        P("node", None),
        P(),
        P(),
        P(),
        P("node", "win", None, None),
    )
    return jax.shard_map(
        body,
        mesh=mesh,
        in_specs=placed,
        out_specs=(P("node", "win", None, None), P("node", None), P()),
        check_vma=False,
    )
```

```python
from functools import partial
import math

import jax
import jax.numpy as jnp
from jax import lax
from jax.experimental import pallas as pl
from jax.experimental.pallas import tpu as pltpu
from jax.sharding import PartitionSpec as P


BLOCK = 128
HALO = 3
KEEP_INPUT = 0.05
F32 = jnp.float32
BF16 = jnp.bfloat16
NT = (((1,), (1,)), ((), ()))
TN = (((0,), (0,)), ((), ()))


def block_diagonal(projections):
    zero = jnp.zeros_like(projections[0])
    return jnp.concatenate(
        [
            jnp.concatenate([projections[0], zero], axis=1),
            jnp.concatenate([zero, projections[1]], axis=1),
        ],
        axis=0,
    )


def split_product(left, right, dims):
    (left_axis,), (right_axis,) = dims[0]
    high, other = left.astype(BF16), right.astype(BF16)
    low = (left - high.astype(F32)).astype(BF16)
    rest = (right - other.astype(F32)).astype(BF16)
    return lax.dot_general(
        jnp.concatenate([high, high, low], axis=left_axis),
        jnp.concatenate([other, rest, other], axis=right_axis),
        dims,
        preferred_element_type=F32,
    )


def pack_kernel(
    x_hbm, g_hbm, nv_hbm, proj_hbm, mix_hbm, own_ref, far_ref, near_ref, m_ref, proj_ref, mix_ref,
    x_in, g_in, nv_in, flat_ref, sems,
):
    copies = [
        pltpu.make_async_copy(source, target, sems.at[i])
        for i, (source, target) in enumerate(
            (
                (x_hbm, x_in),
                (g_hbm, g_in),
                (nv_hbm, nv_in),
                (proj_hbm, proj_ref),
                (mix_hbm, mix_ref),
            )
        )
    ]
    for copy in copies:
        copy.start()
    nodes, width = m_ref.shape
    rim = far_ref.shape[0]
    for part, source in enumerate((x_in, g_in)):
        copies[part].wait()
        flat_ref[...] = source[...].astype(F32)
        for step in range(2):
            rows = flat_ref[pl.ds(step, nodes, stride=2), :].astype(BF16)
            first = (1 + 2 * part + step) * width
            own_ref[:, first : first + width] = rows
    copies[2].wait()
    copies[3].wait()
    learned = jnp.tanh(
        3.0 * split_product(nv_in[...], block_diagonal(proj_ref[...]), (((1,), (0,)), ((), ())))
    )
    m_ref[...] = learned
    own_ref[:, :width] = learned.astype(BF16)
    odd = lax.rem(lax.axis_index("node"), 2)
    gap = nodes - rim
    far_ref[...] = own_ref[pl.ds(pl.multiple_of(odd * gap, BLOCK), rim), :]
    near_ref[...] = own_ref[pl.ds(pl.multiple_of((1 - odd) * gap, BLOCK), rim), :]
    copies[4].wait()


def unit_rows(first, count=1):
    return slice(first * BLOCK, (first + count) * BLOCK)


def rim_places(rim, nodes):
    odd = lax.rem(lax.axis_index("node"), 2)
    span = rim + nodes
    return (
        pl.ds(pl.multiple_of(odd * span, BLOCK), rim),
        pl.ds(pl.multiple_of((1 - odd) * span, BLOCK), rim),
    )


def beside(left, right):
    return jnp.concatenate([left, right], axis=1)


def twice(values):
    return beside(values, values)


def turned(learned):
    width = learned.shape[1]
    half = width // 2
    i = lax.broadcasted_iota(jnp.int32, (width, width), 0)
    j = lax.broadcasted_iota(jnp.int32, (width, width), 1)
    turn = jnp.where(i == j + half, 1.0, 0.0) - jnp.where(j == i + half, 1.0, 0.0)
    return jnp.dot(learned, turn.astype(BF16), preferred_element_type=F32).astype(BF16)


def layer_kernel(
    norm_scale,
    region_ref,
    first_ref,
    far_ref,
    near_ref,
    own_ref,
    m_ref,
    proj_ref,
    mix_ref,
    out_hbm,
    sums_ref,
    x_ref,
    g_ref,
    learned_ref,
    swapped_ref,
    adj_ref,
    adjt_ref,
    score_ref,
    rdeg_ref,
    one_ref,
    two_ref,
    q_one_ref,
    q_two_ref,
    back_ref,
    off_ref,
    offrow_ref,
    dm_ref,
    flat_ref,
    out_ref,
    sem,
):
    b = BLOCK
    nodes = own_ref.shape[0]
    rim, width = far_ref.shape[0], m_ref.shape[1]
    own_units = nodes // b
    units = own_units + 2 * HALO
    reach = HALO + 1
    row = 2 * width
    keep = 1.0 - KEEP_INPUT
    far_place, near_place = rim_places(rim, nodes)
    own_place = pl.ds(rim, nodes)
    for place, source in ((far_place, far_ref), (own_place, own_ref), (near_place, near_ref)):
        learned = source[:, :width]
        learned_ref[place, :] = learned
        swapped_ref[place, :] = turned(learned)
        x_ref[place, :] = source[:, width : width + row]
        g_ref[place, :] = source[:, width + row :]

    firsts = [first_ref[u] for u in range(units)]
    windows = [pl.ds(pl.multiple_of(firsts[u] * b, b), reach * b) for u in range(units)]
    own_first = HALO
    own_last = own_first + own_units
    mixed = jnp.concatenate([mix_ref[2], mix_ref[1]], axis=0)
    for u in range(units):
        rows = unit_rows(u)
        mine = region_ref[u]
        total = jnp.zeros((b, b), F32)
        for k in range(0, reach, 2):
            other = firsts[u] + k
            pair_scores = lax.dot_general(
                learned_ref[rows, :],
                swapped_ref[pl.ds(pl.multiple_of(other * b, b), 2 * b), :],
                NT,
                preferred_element_type=F32,
            )
            for i in range(2):
                same = jnp.where((region_ref[other + i] == mine) & (mine >= 0), 3.0, 0.0)
                squashed = jnp.tanh(pair_scores[:, i * b : (i + 1) * b] * same)
                positive = jnp.maximum(squashed, 0.0)
                negative = jnp.minimum(squashed, 0.0)
                forward = positive * positive
                columns = unit_rows(k + i)
                if own_first <= u < own_last:
                    score_ref[unit_rows(u - own_first), columns] = squashed
                adj_ref[rows, columns] = forward.astype(BF16)
                adjt_ref[rows, columns] = (negative * negative).astype(BF16)
                total = total + forward
        degree = 1.0 + jnp.sum(total, axis=1, keepdims=True)
        rdeg = jnp.broadcast_to(1.0 / degree, (b, width))
        rdeg_ref[rows, :] = rdeg
        for s in range(2):
            cut = slice(s * width, (s + 1) * width)
            back = lax.dot_general(g_ref[rows, cut], mixed, NT, preferred_element_type=F32)
            q_two_ref[rows, cut] = (keep * back[:, :width] * rdeg).astype(BF16)
            back_ref[rows, cut] = back[:, width:]
    order = list(range(own_first, own_last))
    order += [u for u in range(units) if u not in order]
    for u in order:
        rows = unit_rows(u)
        rdeg = twice(rdeg_ref[rows, :])
        carried = jnp.dot(
            adjt_ref[rows, :], q_two_ref[windows[u], :], preferred_element_type=F32
        )
        mine = x_ref[rows, :].astype(F32)
        prop = jnp.dot(adj_ref[rows, :], x_ref[windows[u], :], preferred_element_type=F32)
        prop = (prop + mine) * rdeg
        one_ref[rows, :] = (KEEP_INPUT * mine + keep * prop).astype(BF16)
        carried = carried + q_two_ref[rows, :].astype(F32)
        grad_one = (keep * (back_ref[rows, :] + carried) * rdeg).astype(BF16)
        q_one_ref[rows, :] = grad_one
        inner = grad_one.astype(F32) * prop
        off_ref[rows, :] = inner[:, :width] + inner[:, width:]

    def second_hop(u):
        rows = unit_rows(u)
        prop = jnp.dot(adj_ref[rows, :], one_ref[windows[u], :], preferred_element_type=F32)
        prop = (prop + one_ref[rows, :].astype(F32)) * twice(rdeg_ref[rows, :])
        inner = q_two_ref[rows, :].astype(F32) * prop
        inner = off_ref[rows, :] + inner[:, :width] + inner[:, width:]
        offset = jnp.broadcast_to(jnp.sum(inner, axis=1, keepdims=True), (b, width))
        off_ref[rows, :] = offset
        offrow_ref[u] = jnp.transpose(offset)[:8]
        if own_first <= u < own_last:
            two_ref[unit_rows(u - own_first), :] = (
                KEEP_INPUT * x_ref[rows, :].astype(F32) + keep * prop
            ).astype(BF16)

    for u in range(own_first, own_last):
        second_hop(u)
    weights = jnp.concatenate([mix_ref[0], mix_ref[1], mix_ref[2]], axis=0)
    all_hops, all_up = [], []
    for s in range(2):
        cut = slice(s * width, (s + 1) * width)
        all_hops.append(
            jnp.concatenate(
                [x_ref[own_place, cut], one_ref[own_place, cut], two_ref[:, cut]], axis=1
            )
        )
        all_up.append(g_ref[own_place, cut])
        flat_ref[pl.ds(s, nodes, stride=2), :] = jnp.dot(
            all_hops[s], weights, preferred_element_type=F32
        )
    out_ref[...] = flat_ref[...].astype(BF16)
    out_copy = pltpu.make_async_copy(out_ref, out_hbm, sem)
    out_copy.start()
    for u in range(units):
        if not own_first <= u < own_last:
            second_hop(u)
    groups = sums_ref.shape[0]
    rows_v = nodes // groups
    rows_w = 3 * width // groups
    weight = norm_scale * lax.dot_general(
        jnp.concatenate(all_hops, axis=0),
        jnp.concatenate(all_up, axis=0),
        TN,
        preferred_element_type=F32,
    )
    for k in range(groups):
        sums_ref[k, rows_v:, :] = weight[k * rows_w : (k + 1) * rows_w].astype(BF16)

    for u in range(own_first, own_last):
        rows = unit_rows(u)
        local = unit_rows(u - own_first)
        grad_m = jnp.zeros((b, width), F32)
        for k in range(0, reach, 2):
            columns = pl.ds(pl.multiple_of((firsts[u] + k) * b, b), 2 * b)
            inner = lax.dot_general(
                beside(q_one_ref[rows, :], q_two_ref[rows, :]),
                beside(x_ref[columns, :], one_ref[columns, :]),
                NT,
                preferred_element_type=F32,
            )
            inner_t = lax.dot_general(
                beside(x_ref[rows, :], one_ref[rows, :]),
                beside(q_one_ref[columns, :], q_two_ref[columns, :]),
                NT,
                preferred_element_type=F32,
            )
            squashed = score_ref[local, unit_rows(k, 2)]
            offset_t = jnp.concatenate(
                [offrow_ref[firsts[u] + k + i, 0:1, :] for i in range(2)], axis=1
            )
            chosen = jnp.where(
                squashed > 0.0, inner - twice(off_ref[rows, :]), inner_t - offset_t
            )
            pair = (6.0 * squashed * (1.0 - squashed * squashed) * chosen).astype(BF16)
            grad_m = grad_m + jnp.dot(
                pair, swapped_ref[columns, :], preferred_element_type=F32
            )
        mine = m_ref[local, :]
        dm_ref[local, :] = 3.0 * (1.0 - mine * mine) * grad_m
    grad = split_product(dm_ref[...], block_diagonal(proj_ref[...]), NT).astype(BF16)
    for k in range(groups):
        sums_ref[k, :rows_v, :] = grad[k * rows_v : (k + 1) * rows_v]
    out_copy.wait()


def finish_kernel(got_ref, vector_hbm, weight_hbm, vector_ref, weight_ref, sems):
    groups = got_ref.shape[0]
    rows_v = vector_ref.shape[0] // groups
    rows_w = weight_ref.shape[0] // groups
    for k in range(groups):
        got = got_ref[k].astype(F32)
        vector_ref[k * rows_v : (k + 1) * rows_v, :] = got[:rows_v]
        weight_ref[k * rows_w : (k + 1) * rows_w, :] = got[rows_v:]
    copies = (
        pltpu.make_async_copy(vector_ref, vector_hbm, sems.at[0]),
        pltpu.make_async_copy(weight_ref, weight_hbm, sems.at[1]),
    )
    for copy in copies:
        copy.start()
    for copy in copies:
        copy.wait()


def device_groups(counts, kept):
    strides = [math.prod(counts[i + 1 :]) for i in range(len(counts))]

    def spread(axes):
        numbers = [0]
        for i in axes:
            numbers = [n + k * strides[i] for n in numbers for k in range(counts[i])]
        return numbers

    others = [i for i in range(len(counts)) if i not in kept]
    return [[base + k for k in spread(kept)] for base in spread(others)]


def body(features, node_vectors, projections, mix_weight, region_sizes, cotangent):
    nodes, _, steps, width = features.shape
    axes = ("node", "win")
    node_count, win_count = lax.axis_size("node"), lax.axis_size("win")
    own_units = nodes // BLOCK
    units = own_units + 2 * HALO
    rim = HALO * BLOCK
    flat = nodes * steps
    row = steps * width
    in_vmem = pl.BlockSpec(memory_space=pltpu.VMEM)
    in_hbm = pl.BlockSpec(memory_space=pltpu.HBM)
    features, cotangent = features.reshape(flat, width), cotangent.reshape(flat, width)
    features, cotangent, node_vectors, projections, mix_weight = (
        pltpu.with_memory_space_constraint(array, pltpu.HBM)
        for array in (features, cotangent, node_vectors, projections, mix_weight)
    )
    own, far, near, learned, projections, mix_weight = pl.pallas_call(
        pack_kernel,
        name="pack",
        in_specs=[in_hbm] * 5,
        out_shape=(
            jax.ShapeDtypeStruct((nodes, 5 * width), BF16),
            jax.ShapeDtypeStruct((rim, 5 * width), BF16),
            jax.ShapeDtypeStruct((rim, 5 * width), BF16),
            jax.ShapeDtypeStruct((nodes, width), F32),
            jax.ShapeDtypeStruct(projections.shape, F32),
            jax.ShapeDtypeStruct(mix_weight.shape, BF16),
        ),
        scratch_shapes=[
            pltpu.VMEM((flat, width), BF16),
            pltpu.VMEM((flat, width), BF16),
            pltpu.VMEM((nodes, width), F32),
            pltpu.VMEM((flat, width), F32),
            pltpu.SemaphoreType.DMA((5,)),
        ],
        compiler_params=pltpu.CompilerParams(vmem_limit_bytes=16 << 20),
    )(features, cotangent, node_vectors, projections, mix_weight)
    border = [(i, i + 1) for i in range(1, node_count - 1, 2)]
    inside = [(i, i + 1) for i in range(0, node_count, 2)]
    far = lax.ppermute(far, "node", border + [(j, i) for i, j in border])
    near = lax.ppermute(near, "node", inside + [(j, i) for i, j in inside])
    lead = lax.axis_index("node") * own_units - HALO
    place = jnp.arange(units, dtype=jnp.int32)
    unit = lead + place
    ends = jnp.cumsum(region_sizes)
    passed = (ends[None, :] <= unit[:, None]).astype(jnp.int32)
    in_range = (unit >= 0) & (unit < node_count * own_units)
    region = jnp.where(in_range, jnp.sum(passed, axis=1), -1)
    first = jnp.sum(passed * region_sizes[None, :], axis=1) - lead
    first = jnp.clip(first, jnp.maximum(place - HALO, 0), jnp.minimum(place, units - HALO - 1))

    span = units * BLOCK
    y_far, y_near = 4, 1
    inner_count = node_count // (y_far * y_near)
    groups = y_far * win_count
    rows_v = nodes // groups
    rows_w = 3 * width // groups
    reach = (HALO + 1) * BLOCK
    in_smem = pl.BlockSpec(memory_space=pltpu.SMEM)
    out, sums = pl.pallas_call(
        partial(layer_kernel, 1.0 / math.sqrt(flat * node_count * win_count)),
        name="layer",
        in_specs=[in_smem] * 2 + [in_vmem] * 6,
        out_specs=(in_hbm, in_vmem),
        out_shape=(
            jax.ShapeDtypeStruct((flat, width), BF16),
            jax.ShapeDtypeStruct((groups, rows_v + rows_w, width), BF16),
        ),
        scratch_shapes=[
            pltpu.VMEM((span, row), BF16),
            pltpu.VMEM((span, row), BF16),
            pltpu.VMEM((span, width), BF16),
            pltpu.VMEM((span, width), BF16),
            pltpu.VMEM((span, reach), BF16),
            pltpu.VMEM((span, reach), BF16),
            pltpu.VMEM((nodes, reach), F32),
            pltpu.VMEM((span, width), F32),
            pltpu.VMEM((span, row), BF16),
            pltpu.VMEM((nodes, row), BF16),
            pltpu.VMEM((span, row), BF16),
            pltpu.VMEM((span, row), BF16),
            pltpu.VMEM((span, row), F32),
            pltpu.VMEM((span, width), F32),
            pltpu.VMEM((units, 8, width), F32),
            pltpu.VMEM((nodes, width), F32),
            pltpu.VMEM((flat, width), F32),
            pltpu.VMEM((flat, width), BF16),
            pltpu.SemaphoreType.DMA,
        ],
        compiler_params=pltpu.CompilerParams(vmem_limit_bytes=32 << 20),
        cost_estimate=pl.CostEstimate(
            flops=12 * span * reach * row, bytes_accessed=8 << 20, transcendentals=span * reach
        ),
    )(region, first, far, near, own, learned, projections, mix_weight)

    counts = (y_far, y_near, inner_count, win_count)
    outer_groups = device_groups(counts, (0, 3))
    inner_groups = device_groups(counts, (1, 2))
    exchange = partial(
        lax.all_to_all, axis_name=axes, split_axis=0, concat_axis=0, tiled=True
    )
    got = exchange(sums, axis_index_groups=outer_groups).astype(F32)
    vector_sum = jnp.sum(
        got[:, :rows_v].reshape(y_far, win_count, rows_v, width), axis=1
    ).astype(BF16)
    weight_sum = jnp.sum(got[:, rows_v:], axis=0).astype(BF16)
    shares = jnp.broadcast_to(weight_sum[None], (y_near * inner_count, rows_w, width))
    vector_sum, shares = lax.optimization_barrier((vector_sum, shares))
    got = exchange(shares, axis_index_groups=inner_groups).astype(F32)
    weight_sum = jnp.sum(got, axis=0).astype(BF16)
    back = jnp.concatenate(
        [
            jnp.broadcast_to(
                vector_sum[:, None], (y_far, win_count, rows_v, width)
            ).reshape(groups, rows_v, width),
            jnp.broadcast_to(weight_sum[None], (groups, rows_w, width)),
        ],
        axis=1,
    )
    got = exchange(back, axis_index_groups=outer_groups)
    vector_grad, weight_grad = pl.pallas_call(
        finish_kernel,
        name="finish",
        in_specs=[in_vmem],
        out_shape=(
            jax.ShapeDtypeStruct((nodes, width), F32),
            jax.ShapeDtypeStruct((3 * width, width), F32),
        ),
        out_specs=(in_hbm, in_hbm),
        scratch_shapes=[
            pltpu.VMEM((nodes, width), F32),
            pltpu.VMEM((3 * width, width), F32),
            pltpu.SemaphoreType.DMA((2,)),
        ],
        compiler_params=pltpu.CompilerParams(vmem_limit_bytes=8 << 20),
    )(got)
    weight_grad = weight_grad.reshape(3, width, width)
    return (out.reshape(nodes, 1, steps, width), vector_grad, weight_grad)


def solution(mesh):
    placed = (
        P("node", "win", None, None),
        P("node", None),
        P(),
        P(),
        P(),
        P("node", "win", None, None),
    )
    return jax.shard_map(
        body,
        mesh=mesh,
        in_specs=placed,
        out_specs=(P("node", "win", None, None), P("node", None), P()),
        check_vma=False,
    )
```
